1024 devices in a mesh: gx: 16 (over z, core), gy: 64 (over x, y).
Axes of the slice: x: 8, y: 8, z: 8, core: 2. Of those that a mesh axis runs over, the one named last changes fastest.
Arguments:
- initial_state: float32 [9, 4, 64, 8192], P(None, None, 'gx', 'gy'), may hold values from -6 to 6
- lame_lambda: float32 [4, 64, 8192], P(None, 'gx', 'gy'), may hold values from 0.5 to 1.5
- shear_modulus: float32 [4, 64, 8192], P(None, 'gx', 'gy'), may hold values from 0.3 to 1
- buoyancy: float32 [4, 64, 8192], P(None, 'gx', 'gy'), may hold values from 0.5 to 1
- source_cells: int32 [65536], P(('gx', 'gy')), may hold values from 0 to 2047
- source_wavelet: float32 [3, 65536], P(None, ('gx', 'gy')), may hold values from -8 to 8
- segment_start: int32 [2097152], P(('gx', 'gy')), may hold values from 0 to 1935
- segment_weight: float32 [2, 2097152], P(None, ('gx', 'gy')), may hold values from 0.2 to 1
- partial_owner: int32 [2097152, 1], P(('gx', 'gy')), may hold values from 0 to 1023; in each aligned block of 2048 rows (0 to 2047, 2048 to 4095, ...) at most 4 rows name the same one
- partial_channel: int32 [2097152], P(('gx', 'gy')), may hold values from 0 to 1023
- observed_data: float32 [3, 1048576], P(None, ('gx', 'gy')), may hold values from -6 to 6
Outputs:
- residuals: float32 [3, 1048576], P(None, ('gx', 'gy'))
- gradients: float32 [2, 4, 64, 8192], P(None, None, 'gx', 'gy')
The draws below stay inside these ranges and needn't reach their ends.
Inputs may be any that keep to these rules, and one draw needn't show every extreme that they name: `partial_owner`: each row names the device that owns the segment's channel, counted with gx slowest; the rows of one device name one owner at most 4 times. `partial_channel`: the segment's channel among its owner's 1024 channels. `segment_start`: index of the segment's first cell in its device's grid of starts of shape [4, 4, 121], flattened in that order. `source_cells`: index of the source's cell in its device's tile of shape [4, 4, 128], flattened in that order; cells may repeat.
All inputs are finite; a program needn't handle non-finite values.
Results may differ from the reference program's by a relative error of at most 0.00002.
Values sent between devices are 32-bit elements; how exact they have to be, the bound alone decides.
A program may use at most 32 MiB of HBM per device.

```python
import math
import jax
import jax.numpy as jnp
import numpy as np

NZ = 4
CX = 4
CY = 128
STEPS = 3
GAUGE = 8
PART_DEV = 2048
CH_DEV = 1024
SRC_DEV = 64
NX = 64
NY = 8192
CAP = 4
PART_TOTAL = 2097152
CHANNELS = 1048576
SRC_TOTAL = 65536
N_GY = 64
DEVICES = 1024


def touch_ends(array, rng, low, high):
    spot = [jax.random.randint(jax.random.fold_in(rng, axis), (), 0, length) for axis, length in enumerate(array.shape)]
    widest = array.shape.index(max(array.shape))
    next_to = spot[:widest] + [(spot[widest] + 1) % array.shape[widest]] + spot[widest + 1:]
    return array.at[tuple(spot)].set(low).at[tuple(next_to)].set(high)


def level_of(own_key, dims, pieces, smallest, top_value):
    loudness, own = 1.0, jax.random.fold_in(own_key, 6)
    for dim, blocks in pieces:
        draws = jnp.exp(jax.random.uniform(jax.random.fold_in(own, dim), (blocks,), jnp.float32, smallest / len(pieces), top_value / len(pieces)))
        loudness = loudness * jnp.repeat(draws, dims[dim] // blocks).reshape([-1 if axis == dim else 1 for axis in range(len(dims))])
    return loudness


def deal_out(own_key, own, number, rows, amount, top, limit, slope):
    order = jax.random.permutation(own_key, amount)
    packed, common = portions_of(amount, rows * top, limit, slope, True), portions_of(amount, rows * top, limit, slope, False)
    places = jnp.arange(amount)

    def named(lengths, offset_by):
        used = int((lengths > 0).sum())
        fixed = max(1, used // 4)
        passed = fixed + (places - fixed + offset_by * (used - fixed)) % max(1, amount - fixed)
        return jnp.zeros((amount,), jnp.int32).at[order[jnp.where(places < fixed, places, passed)]].set(jnp.asarray(lengths, jnp.int32))

    lengths = jnp.where(number % 4 == 0, named(packed, number // 4), named(common, number - number // 4 - 1))
    mixed = jax.random.permutation(jax.random.fold_in(own, 3), amount)
    source_of, receiver = mixed[0:amount // 2 * 2:2], mixed[1:amount // 2 * 2:2]
    room = jnp.minimum(lengths[source_of] - 1, limit - lengths[receiver]) // 2
    room = jnp.where((source_of == order[0]) | (receiver == order[0]) | (lengths[receiver] == 0), 0, jnp.maximum(room, 0))
    passed = jax.random.randint(jax.random.fold_in(own, 4), (amount // 2,), 0, 1 << 20) % (room + 1)
    lengths = lengths.at[source_of].add(-passed).at[receiver].add(passed)
    members = jnp.searchsorted(jnp.cumsum(lengths), jnp.arange(rows * top), side="right").astype(jnp.int32)
    listing = members.reshape(top, rows).T
    listing = listing[jax.random.permutation(jax.random.fold_in(own, 1), rows)]
    offset_by = jax.random.randint(jax.random.fold_in(own, 2), (rows, 1), 0, top)
    return jnp.take_along_axis(listing, (jnp.arange(top)[None, :] + offset_by) % top, axis=1)


def portions_of(count, total, most, slope, full):
    loads = [(1 << 20) // math.isqrt(rank ** slope) + 1 for rank in range(1, count + 1)]
    largest = most if full else min(most, max(-(-total // count), total * loads[0] // sum(loads)))
    least = 1 if total - largest >= count - 1 else 0
    holding, spare = [largest] + [least] * (count - 1), total - largest - least * (count - 1)
    while spare > 0:
        movable = [i for i in range(1, count) if holding[i] < largest] or [i for i in range(1, count) if holding[i] < most]
        whole, left = sum([loads[i] for i in movable]), spare
        for i in movable:
            more = min(most - holding[i], max(1, left * loads[i] // whole), spare)
            holding[i] = holding[i] + more
            spare = spare - more
    return np.array(holding)


def noise(rng, shape, width, most, pieces=(), kind=jnp.bfloat16):
    result = width * jax.random.normal(rng, shape, jnp.float32)
    if pieces:
        result = result * level_of(rng, shape, pieces, -0.22, 0.18)
    return jnp.clip(result, -most, most).astype(kind)


def setup_inputs(seed: int = 0) -> dict:
    seeds = jax.random.split(jax.random.key(seed), 12)
    initial_state = noise(seeds[0], (9, NZ, NX, NY), 1.0, 6.0, ((2, 16), (3, 64)), jnp.float32)
    lame_lambda = jnp.clip(0.5 + 1.0 * jax.random.uniform(seeds[1], (NZ, NX, NY), jnp.float32) ** level_of(seeds[1], (NZ, NX, NY), ((1, 16), (2, 64)), -0.2, 0.2), 0.5, 1.5)
    shear_modulus = jnp.clip(0.3 + 0.7 * jax.random.uniform(seeds[2], (NZ, NX, NY), jnp.float32) ** level_of(seeds[2], (NZ, NX, NY), ((1, 16), (2, 64)), -0.2, 0.2), 0.3, 1.0)
    buoyancy = jnp.clip(0.5 + 0.5 * jax.random.uniform(seeds[3], (NZ, NX, NY), jnp.float32) ** level_of(seeds[3], (NZ, NX, NY), ((1, 16), (2, 64)), -0.2, 0.2), 0.5, 1.0)
    source_cells = touch_ends(jax.random.randint(seeds[4], (SRC_TOTAL,), 0, NZ * CX * CY), jax.random.fold_in(seeds[4], 1), 0, (NZ * CX * CY) - 1).astype(jnp.int32)
    source_wavelet = noise(seeds[5], (STEPS, SRC_TOTAL), 2.0, 8.0, ((1, 1024),), jnp.float32)
    segment_start = touch_ends(jax.random.randint(seeds[6], (PART_TOTAL,), 0, NZ * CX * (CY - GAUGE + 1)), jax.random.fold_in(seeds[6], 1), 0, (NZ * CX * (CY - GAUGE + 1)) - 1).astype(jnp.int32)
    segment_weight = jnp.clip(0.2 + 0.8 * jax.random.uniform(seeds[7], (2, PART_TOTAL), jnp.float32) ** level_of(seeds[7], (2, PART_TOTAL), ((1, 1024),), -0.2, 0.2), 0.2, 1.0)
    partial_owner_keys = jax.random.split(jax.random.fold_in(seeds[8], 1), PART_TOTAL // PART_DEV)
    partial_owner_turns = jax.random.permutation(jax.random.fold_in(seeds[8], 3), PART_TOTAL // PART_DEV)
    partial_owner = jax.vmap(lambda own, number: deal_out(jax.random.fold_in(seeds[8], 2), own, number, PART_DEV, DEVICES, 1, CAP, 2))(partial_owner_keys, partial_owner_turns).reshape((PART_TOTAL, 1))
    partial_channel = touch_ends(jax.random.randint(seeds[9], (PART_TOTAL,), 0, CH_DEV), jax.random.fold_in(seeds[9], 1), 0, CH_DEV - 1).astype(jnp.int32)
    observed_data = noise(seeds[10], (STEPS, CHANNELS), 1.0, 6.0, ((1, 1024),), jnp.float32)
    return {"initial_state": initial_state, "lame_lambda": lame_lambda, "shear_modulus": shear_modulus, "buoyancy": buoyancy, "source_cells": source_cells, "source_wavelet": source_wavelet, "segment_start": segment_start, "segment_weight": segment_weight, "partial_owner": partial_owner, "partial_channel": partial_channel, "observed_data": observed_data}


time_step = 0.25


def crop_rim(values):
    return values[..., 1:-1, 1:-1]


def ahead_x(values):
    return values[..., 2:, 1:-1] - values[..., 1:-1, 1:-1]


def behind_x(values):
    return values[..., 1:-1, 1:-1] - values[..., :-2, 1:-1]


def ahead_y(values):
    return values[..., 1:-1, 2:] - values[..., 1:-1, 1:-1]


def behind_y(values):
    return values[..., 1:-1, 1:-1] - values[..., 1:-1, :-2]


def ahead_z(inner_part):
    return jnp.concatenate([inner_part[..., 1:, :, :], jnp.zeros_like(inner_part[..., :1, :, :])], axis=-3) - inner_part


def behind_z(inner_part):
    return inner_part - jnp.concatenate([jnp.zeros_like(inner_part[..., :1, :, :]), inner_part[..., :-1, :, :]], axis=-3)


def velocity_update(velocity, stress_pad, buoyancy):
    accel_x = ahead_x(stress_pad[0]) + behind_y(stress_pad[3]) + behind_z(crop_rim(stress_pad[4]))
    accel_y = behind_x(stress_pad[3]) + ahead_y(stress_pad[1]) + behind_z(crop_rim(stress_pad[5]))
    accel_z = behind_x(stress_pad[4]) + behind_y(stress_pad[5]) + ahead_z(crop_rim(stress_pad[2]))
    return velocity + time_step * buoyancy * jnp.stack([accel_x, accel_y, accel_z])


def strain_rates(velocity_pad):
    along_x = velocity_pad[0]
    along_y = velocity_pad[1]
    along_z = velocity_pad[2]
    return jnp.stack([behind_x(along_x), behind_y(along_y), behind_z(crop_rim(along_z)),
                      ahead_y(along_x) + ahead_x(along_y),
                      ahead_z(crop_rim(along_x)) + ahead_x(along_z),
                      ahead_z(crop_rim(along_y)) + ahead_y(along_z)])


def stress_update(stress, strains, lame_lambda, shear_modulus):
    dilation = strains[0] + strains[1] + strains[2]
    normal = stress[:3] + time_step * (lame_lambda * dilation + 2.0 * shear_modulus * strains[:3])
    sheared = stress[3:] + time_step * shear_modulus * strains[3:]
    return jnp.concatenate([normal, sheared])


def gradient_terms(forward, adjoint):
    products = forward * adjoint
    lambda_term = (forward[0] + forward[1] + forward[2]) * (adjoint[0] + adjoint[1] + adjoint[2])
    shear_term = 2.0 * (products[0] + products[1] + products[2]) + products[3] + products[4] + products[5]
    return jnp.stack([lambda_term, shear_term])


def window_sums(values, gauge_len):
    span_len = values.shape[-1] - gauge_len + 1
    running = values[..., 0:span_len]
    for offset in range(1, gauge_len):
        running = running + values[..., offset:offset + span_len]
    return running


def spread_back(values, gauge_len):
    widths = [(0, 0)] * (values.ndim - 1)
    running = jnp.pad(values, widths + [(0, gauge_len - 1)])
    for offset in range(1, gauge_len):
        running = running + jnp.pad(values, widths + [(offset, gauge_len - 1 - offset)])
    return running


def pad_lateral(values):
    return jnp.pad(values, [(0, 0)] * (values.ndim - 2) + [(1, 1), (1, 1)])


def run_step(velocity, stress, lame_lambda, shear_modulus, buoyancy):
    velocity = velocity_update(velocity, pad_lateral(stress), buoyancy)
    strains = strain_rates(pad_lateral(velocity))
    stress = stress_update(stress, strains, lame_lambda, shear_modulus)
    return velocity, stress, strains


def reference(initial_state, lame_lambda, shear_modulus, buoyancy, source_cells, source_wavelet, segment_start, segment_weight, partial_owner, partial_channel, observed_data):
    span_local = CY - GAUGE + 1
    span_global = NY - GAUGE + 1
    src_device = jnp.arange(SRC_TOTAL, dtype=jnp.int32) // SRC_DEV
    src_depth = source_cells // (CX * CY)
    src_rest = source_cells % (CX * CY)
    src_row = (src_device // N_GY) * CX + src_rest // CY
    src_col = (src_device % N_GY) * CY + src_rest % CY
    src_global = ((src_depth * NX + src_row) * NY + src_col).astype(jnp.int32)
    seg_device = jnp.arange(PART_TOTAL, dtype=jnp.int32) // PART_DEV
    seg_depth = segment_start // (CX * span_local)
    seg_rest = segment_start % (CX * span_local)
    seg_row = (seg_device // N_GY) * CX + seg_rest // span_local
    seg_col = (seg_device % N_GY) * CY + seg_rest % span_local
    seg_global = ((seg_depth * NX + seg_row) * span_global + seg_col).astype(jnp.int32)
    velocity = initial_state[:3]
    stress = initial_state[3:]
    forward_strains = []
    partial_rows = []
    for step_index in range(STEPS):
        normal = stress[:3].reshape(3, -1).at[:, src_global].add(source_wavelet[step_index]).reshape(3, NZ, NX, NY)
        stress = jnp.concatenate([normal, stress[3:]])
        velocity, stress, strains = run_step(velocity, stress, lame_lambda, shear_modulus, buoyancy)
        forward_strains.append(strains)
        windows = window_sums(strains[:2], GAUGE).reshape(2, -1)[:, seg_global]
        partial_rows.append(segment_weight[0] * windows[0] + segment_weight[1] * windows[1])
    partials = jnp.stack(partial_rows)
    channel_index = (partial_owner[:, 0] * CH_DEV + partial_channel).astype(jnp.int32)
    channel_sums = jax.ops.segment_sum(partials.T, channel_index, num_segments=CHANNELS).T
    residuals = channel_sums - observed_data
    adj_velocity = jnp.zeros((3, NZ, NX, NY), jnp.float32)
    adj_stress = jnp.zeros((6, NZ, NX, NY), jnp.float32)
    gradients = jnp.zeros((2, NZ, NX, NY), jnp.float32)
    for turn_index in range(STEPS):
        back_values = residuals[STEPS - 1 - turn_index][channel_index]
        load_map = jnp.zeros((2, NZ * NX * span_global), jnp.float32).at[:, seg_global].add(segment_weight * back_values)
        spread = spread_back(load_map.reshape(2, NZ, NX, span_global), GAUGE)
        adj_stress = jnp.concatenate([adj_stress[:2] + spread, adj_stress[2:]])
        adj_velocity, adj_stress, adj_strains = run_step(adj_velocity, adj_stress, lame_lambda, shear_modulus, buoyancy)
        gradients = gradients + gradient_terms(forward_strains[STEPS - 1 - turn_index], adj_strains)
    return residuals, gradients
```

```python
import functools

import jax
import jax.numpy as jnp
from jax import lax
from jax.experimental import pallas as pl
from jax.experimental.pallas import tpu as pltpu
from jax.sharding import PartitionSpec as P

GAUGE = 8
DT = 0.25
PIECES = 3
STEPS = 3
NF = 14
MESH = pl.DeviceIdType.MESH
NT = (((1,), (1,)), ((), ()))
NN = (((1,), (0,)), ((), ()))


def iota(shape, dim):
    return lax.broadcasted_iota(jnp.int32, shape, dim)


def split(x):
    parts = []
    for _ in range(PIECES):
        part = x.astype(jnp.bfloat16)
        parts.append(part)
        x = x - part.astype(jnp.float32)
    return parts


def dot(a, b, dims):
    return lax.dot_general(a, b, dims, preferred_element_type=jnp.float32)


def dot_split(x, b, dims):
    parts = split(x)
    rows = x.shape[0]
    stacked = dot(jnp.concatenate(parts, axis=0), b, dims)
    total = stacked[:rows]
    for i in range(1, PIECES):
        total = total + stacked[i * rows : (i + 1) * rows]
    return total


def ones_where(mask):
    return jnp.where(mask, 1.0, 0.0).astype(jnp.bfloat16)


def ahead(f, axis):
    return pltpu.roll(f, f.shape[axis] - 1, axis) - f


def behind(f, axis):
    return f - pltpu.roll(f, 1, axis)


def time_step(ext, mats, emit):
    def plane(ref, f, z):
        return ref[f, pl.ds(16 * z, 16), :]

    def ahead_z(f, z):
        return (plane(ext, f, z + 1) if z < 3 else 0.0) - plane(ext, f, z)

    def behind_z(f, z):
        here = plane(ext, f, z)
        return here - plane(ext, f, z - 1) if z > 0 else here

    for z in range(4):
        scale = DT * plane(mats, 0, z)
        sxy, sxz, syz = plane(ext, 6, z), plane(ext, 7, z), plane(ext, 8, z)
        ax = ahead(plane(ext, 3, z), 0) + behind(sxy, 1) + behind_z(7, z)
        ay = behind(sxy, 0) + ahead(plane(ext, 4, z), 1) + behind_z(8, z)
        az = behind(sxz, 0) + behind(syz, 1) + ahead_z(5, z)
        for f, a in enumerate((ax, ay, az)):
            ext[f, pl.ds(16 * z, 16), :] = plane(ext, f, z) + scale * a
    for z in range(4):
        vx, vy, vz = plane(ext, 0, z), plane(ext, 1, z), plane(ext, 2, z)
        exx = behind(vx, 0)
        eyy = behind(vy, 1)
        ezz = behind_z(2, z)
        exy = ahead(vx, 1) + ahead(vy, 0)
        exz = ahead_z(0, z) + ahead(vz, 0)
        eyz = ahead_z(1, z) + ahead(vz, 1)
        emit(z, [e[4:8, 0:128] for e in (exx, eyy, ezz, exy, exz, eyz)])
        lam, mu = plane(mats, 1, z), plane(mats, 2, z)
        dil = lam * (exx + eyy + ezz)
        for f, e in ((3, exx), (4, eyy), (5, ezz)):
            ext[f, pl.ds(16 * z, 16), :] = plane(ext, f, z) + DT * (dil + 2.0 * mu * e)
        for f, e in ((6, exy), (7, exz), (8, eyz)):
            ext[f, pl.ds(16 * z, 16), :] = plane(ext, f, z) + DT * mu * e


def kernel(
    ngx,
    ngy,
    npart,
    state,
    lam,
    mu,
    buoy,
    scell,
    swave,
    start,
    weight,
    owner,
    chan,
    obs,
    res_out,
    grad_out,
    own,
    xr,
    strip,
    yr,
    ext,
    mats,
    srcs,
    es,
    ad,
    glhs,
    colb,
    rank,
    win,
    lane1h,
    obs32,
    sa,
    ra,
    sb,
    rb,
    arr,
    chan1h,
    hirow,
    sb2,
    rb2,
    sa2,
    ra2,
    load,
    xr2,
    strip2,
    yr2,
    halo2,
    exl,
    hsend,
    hrecv,
    h2send,
    h2recv,
    esend,
    erecv,
):
    gx, gy = lax.axis_index("gx"), lax.axis_index("gy")
    nchunk = npart // 128
    gy_bits = ngy.bit_length() - 1
    right_x, left_x = lax.rem(gx + 1, ngx), lax.rem(gx + ngx - 1, ngx)
    right_y, left_y = lax.rem(gy + 1, ngy), lax.rem(gy + ngy - 1, ngy)
    first_x, last_x = gx == 0, gx == ngx - 1
    first_y, last_y = gy == 0, gy == ngy - 1

    if ngx < 16 or ngy < 64:
        ra[...] = jnp.zeros_like(ra)
        rb[...] = jnp.zeros_like(rb)
        rb2[...] = jnp.zeros_like(rb2)
        ra2[...] = jnp.zeros_like(ra2)

    barrier = pltpu.get_barrier_semaphore()

    def greet(x, y):
        pl.semaphore_signal(barrier, inc=1, device_id={"gx": x, "gy": y}, device_id_type=MESH)

    for x in (left_x, right_x):
        for y in (left_y, right_y):
            greet(x, y)

    @pl.loop(1, ngx)
    def _(i):
        greet(lax.rem(gx + i, ngx), gy)

    @pl.loop(1, ngy)
    def _(i):
        greet(gx, lax.rem(gy + i, ngy))

    cell = scell[...]
    nsrc = cell.shape[1]
    key = iota((48, nsrc), 0)
    wave = jnp.concatenate([jnp.broadcast_to(swave[t : t + 1, :], (16, nsrc)) for t in range(STEPS)], axis=0)
    lhs = jnp.where((key & 15) == (cell >> 7), wave, 0.0)
    srcs[...] = dot_split(lhs, ones_where(iota((128, nsrc), 0) == (cell & 127)), NT)
    own[0:144, :] = state[...]
    for f in (3, 4, 5):
        own[16 * f : 16 * f + 16, :] = state[16 * f : 16 * f + 16, :] + srcs[0:16, :]
    own[144:160, :] = buoy[...]
    own[160:176, :] = lam[...]
    own[176:192, :] = mu[...]
    own[192:224, :] = srcs[16:48, :]

    lane = iota((8, 128), 1)
    sub = iota((8, 128), 0)
    low4 = (lane & 7) < 4

    def pack(tile_of, groups, put):
        for u in range(-(-groups // 16)):
            acc = [jnp.zeros((8, 128), jnp.float32)] * 2
            for k in range(min(16, groups - 16 * u)):
                tile = tile_of(16 * u + k)
                here = (lane >> 3) == k
                acc[0] = jnp.where(here, pltpu.roll(tile, (8 * k - 124) % 128, 1), acc[0])
                acc[1] = jnp.where(here, pltpu.roll(tile, (8 * k + 4) % 128, 1), acc[1])
            for side in range(2):
                put(side, u, acc[side])

    def put_strip(side, u, value):
        strip[side, pl.ds(8 * u, 8), :] = value

    pack(lambda i: own[8 * i : 8 * i + 8, :], 2 * NF, put_strip)

    ownf = owner[...].astype(jnp.float32)
    cols = jnp.concatenate([ownf, jnp.zeros((128 - nchunk, 128), jnp.float32)], axis=0).T
    for c in range(nchunk):
        colb[c] = jnp.broadcast_to(cols[:, c : c + 1], (128, 128))
    earlier = iota((128, 128), 0) < iota((128, 128), 1)

    @pl.loop(0, nchunk)
    def _(c):
        row = jnp.broadcast_to(owner[pl.ds(c, 1), :].astype(jnp.float32), (128, 128))
        same = jnp.where((colb[c] == row) & earlier, 1.0, 0.0)

        def more(q, count):
            hit = jnp.where(colb[q] == row, 1.0, 0.0)
            return count + hit.reshape(16, 8, 128).sum(axis=0)

        count = lax.fori_loop(0, c, more, same.reshape(16, 8, 128).sum(axis=0))
        rank[pl.ds(c, 1), :] = jnp.sum(count, axis=0, keepdims=True)

    mats[...] = jnp.zeros_like(mats)
    ext[...] = jnp.zeros_like(ext)
    exl[...] = jnp.zeros_like(exl)
    glhs[...] = jnp.zeros_like(glhs)
    obs32[...] = jnp.zeros_like(obs32)
    for i in range(8):
        obs32[4 * i : 4 * i + 3, :] = obs[:, 128 * i : 128 * i + 128]

    pl.semaphore_wait(barrier, ngx - 1 + ngy - 1 + 4)

    def halo_copies(rows, rows_to, strips, strips_to, send, recv):
        plan = [
            (rows, rows_to.at[0], right_x, gy),
            (rows, rows_to.at[1], left_x, gy),
            (strips.at[0], strips_to.at[1, 0], gx, right_y),
            (strips.at[1], strips_to.at[1, 1], gx, left_y),
            (strips.at[0], strips_to.at[0, 0], right_x, right_y),
            (strips.at[1], strips_to.at[0, 1], right_x, left_y),
            (strips.at[0], strips_to.at[2, 0], left_x, right_y),
            (strips.at[1], strips_to.at[2, 1], left_x, left_y),
        ]
        copies = [
            pltpu.make_async_remote_copy(
                src_ref=src,
                dst_ref=dst,
                send_sem=send.at[i],
                recv_sem=recv.at[i],
                device_id={"gx": x, "gy": y},
                device_id_type=MESH,
            )
            for i, (src, dst, x, y) in enumerate(plan)
        ]
        for copy in copies:
            copy.start()
        return copies

    copies = halo_copies(own, xr, strip, yr, hsend, hrecv)

    def chunk_key(c, width):
        own_c = jnp.concatenate([owner[c + i : c + i + 1, :] for i in range(width)], axis=1)
        rank_c = jnp.concatenate([rank[c + i : c + i + 1, :] for i in range(width)], axis=1).astype(jnp.int32)
        return own_c, rank_c

    def row_of(c, width):
        start_c = jnp.concatenate([start[c + i : c + i + 1, :] for i in range(width)], axis=1)
        row_c = (start_c * 8666) >> 20
        return start_c, row_c

    for c in range(nchunk):
        start_c, row_c = row_of(c, 1)
        ahead_c = iota((128, 128), 0) - (start_c - 121 * row_c)
        win[:, 128 * c : 128 * c + 128] = ones_where((ahead_c >= 0) & (ahead_c < GAUGE))
        own_c, rank_c = chunk_key(c, 1)
        lane_c = (own_c & (ngy - 1)) * 2 + (rank_c & 1)
        lane1h[:, 128 * c : 128 * c + 128] = ones_where(iota((128, 128), 0) == lane_c)

    def place_rows(g, rows_ref, drop):
        for f in range(NF):
            for z in range(4):
                part = rows_ref[16 * f + 4 * z : 16 * f + 4 * z + 4, :]
                if drop is not None:
                    part = jnp.where(drop, 0.0, part)
                put_ext(f, slice(16 * z + 4 * g, 16 * z + 4 * g + 4), slice(0, 128), part)

    def put_ext(f, rows, lanes, value):
        if f < 9:
            ext[f, rows, lanes] = value
        elif f < 12:
            mats[f - 9, rows, lanes] = value
        else:
            exl[f - 12, rows, lanes] = value

    def comb(strips, g, u):
        low = jnp.where(first_y, 0.0, strips[g, 0, pl.ds(8 * u, 8), :])
        high = jnp.where(last_y, 0.0, strips[g, 1, pl.ds(8 * u, 8), :])
        both = jnp.where(low4, low, high)
        if g == 0:
            both = jnp.where(first_x, 0.0, both)
        if g == 2:
            both = jnp.where(last_x, 0.0, both)
        return both

    place_rows(1, own, None)
    for copy in copies:
        copy.wait()
    place_rows(0, xr.at[0], first_x)
    place_rows(2, xr.at[1], last_x)
    for g in range(3):
        for u in range(2):
            both = comb(yr, g, u)
            for k in range(min(16, 2 * NF - 16 * u)):
                f, h = divmod(16 * u + k, 2)
                tile = pltpu.roll(both, (124 - 8 * k) % 128, 1)
                for i in range(2):
                    z = 2 * h + i
                    put_ext(f, slice(16 * z + 4 * g, 16 * z + 4 * g + 4), slice(128, 256), tile[4 * i : 4 * i + 4, :])

    for t in range(STEPS):
        if t > 0:
            for f in (3, 4, 5):
                ext[f] = ext[f] + exl[t - 1]

        def emit(z, e, t=t):
            for i in range(6):
                es[6 * t + i, pl.ds(4 * z, 4), :] = e[i]
            for f in range(2):
                glhs[pl.ds(32 * z + 4 * f + t, 4, stride=8), :] = e[f]

        time_step(ext, mats, emit)

    def sub_of(width):
        return iota((8, width), 0)

    def weights(c, width):
        both = weight[:, 128 * c : 128 * (c + width)]
        return jnp.where(sub_of(128 * width) < 4, both[0:1, :], both[1:2, :])

    width = 2 if nchunk % 2 == 0 else 1
    wide = 128 * width
    gpieces = jnp.concatenate(split(glhs[...]), axis=0)
    acc = jnp.zeros((PIECES * 128, 128), jnp.float32)
    for c in range(0, nchunk, width):
        lanes = slice(128 * c, 128 * c + wide)
        _, row_c = row_of(c, width)
        got = dot(gpieces, win[:, lanes], NN)
        picked = jnp.zeros((8, wide), jnp.float32)
        for r in range(16):
            tile = got[8 * r : 8 * r + 8]
            for i in range(1, PIECES):
                tile = tile + got[128 * i + 8 * r : 128 * i + 8 * r + 8]
            picked = picked + jnp.where(row_c == r, tile, 0.0)
        picked = picked * weights(c, width)
        picked = picked + pltpu.roll(picked, 4, 0)
        chan_c = jnp.concatenate([chan[c + i : c + i + 1, :] for i in range(width)], axis=1)
        picked = jnp.where((sub_of(wide) & 3) == 3, chan_c.astype(jnp.float32), picked)
        own_c, rank_c = chunk_key(c, width)
        key_c = (own_c >> gy_bits) * 2 + (rank_c >> 1)
        hit = (iota((128, wide), 0) >> 2) == key_c
        parts = [
            jnp.where(hit, jnp.concatenate([part.astype(jnp.float32)] * 16, axis=0), 0.0).astype(jnp.bfloat16)
            for part in split(picked)
        ]
        acc = acc + dot(jnp.concatenate(parts, axis=0), lane1h[:, lanes], NT)
    total = acc[0:128]
    for i in range(1, PIECES):
        total = total + acc[128 * i : 128 * i + 128]
    sa[...] = total.reshape(16, 8, 128)

    def exchange(stage, src, dst, count, axis, me):
        unit = src.shape[0] // (16 if axis == "gx" else 64)
        send, recv = esend.at[stage], erecv.at[stage]
        other = "gy" if axis == "gx" else "gx"
        there = gy if axis == "gx" else gx

        def part(ref, i):
            return ref.at[pl.ds(i * unit, unit)]

        mine = pltpu.make_async_copy(part(src, me), part(dst, me), recv)
        mine.start()

        @pl.loop(1, count)
        def _(i):
            to = lax.rem(me + i, count)
            pltpu.make_async_remote_copy(
                src_ref=part(src, to),
                dst_ref=part(dst, me),
                send_sem=send,
                recv_sem=recv,
                device_id={axis: to, other: there},
                device_id_type=MESH,
            ).start()

        whole = dst.at[pl.ds(0, count * unit)]
        pltpu.make_async_copy(whole, whole, recv).wait()
        less = src.at[pl.ds(0, (count - 1) * unit)]
        pltpu.make_async_copy(less, less, send).wait()

    exchange(0, sa, ra, ngx, "gx", gx)
    sb[...] = ra[...].reshape(128, 128).T.reshape(64, 2, 128)
    exchange(1, sb, rb, ngy, "gy", gy)
    arr[...] = rb[...].reshape(128, 128).T

    acc = jnp.zeros((PIECES * 32, 128), jnp.float32)
    sub256 = sub_of(256) >> 2
    for d in range(16):
        tile = arr[8 * d : 8 * d + 8, :]
        turned = pltpu.roll(tile, 4, 0)
        both = jnp.concatenate([jnp.where(sub < 4, tile, turned), jnp.where(sub < 4, turned, tile)], axis=1)
        ids = both[3:4, :].astype(jnp.int32)
        onehot = ones_where(iota((128, 256), 0) == (ids & 127))
        chan1h[:, 256 * d : 256 * d + 256] = onehot
        hi = ids >> 7
        hirow[d : d + 1, :] = hi
        parts = []
        for part in split(both):
            part = part.astype(jnp.float32)
            for j in range(4):
                parts.append(jnp.where(hi == sub256 + 2 * j, part, 0.0).astype(jnp.bfloat16))
        acc = acc + dot(jnp.concatenate(parts, axis=0), onehot, NT)
    sums = acc[0:32]
    for i in range(1, PIECES):
        sums = sums + acc[32 * i : 32 * i + 32]
    sums = jnp.where((iota((32, 128), 0) & 3) == 3, 0.0, sums - obs32[...])
    for i in range(8):
        res_out[:, 128 * i : 128 * i + 128] = sums[4 * i : 4 * i + 3, :]

    pieces = jnp.concatenate(split(sums), axis=0)
    for d in range(16):
        got = dot(pieces, chan1h[:, 256 * d : 256 * d + 256], NN)
        hi = hirow[d : d + 1, :]
        picked = jnp.zeros((8, 256), jnp.float32)
        for j in range(4):
            tile = got[8 * j : 8 * j + 8]
            for i in range(1, PIECES):
                tile = tile + got[32 * i + 8 * j : 32 * i + 8 * j + 8]
            picked = picked + jnp.where(hi == sub256 + 2 * j, tile, 0.0)
        picked = picked + pltpu.roll(picked, 4, 0)
        arr[8 * d : 8 * d + 8, :] = jnp.where(sub < 4, picked[:, 0:128], picked[:, 128:256])
    sb2[...] = arr[...].T.reshape(64, 2, 128)
    exchange(2, sb2, rb2, ngy, "gy", gy)
    sa2[...] = rb2[...].reshape(128, 128).T.reshape(16, 8, 128)
    exchange(3, sa2, ra2, ngx, "gx", gx)

    pieces = jnp.concatenate(split(ra2[...].reshape(128, 128)), axis=0)
    acc = jnp.zeros((PIECES * 128, 128), jnp.float32)
    for c in range(0, nchunk, width):
        lanes = slice(128 * c, 128 * c + wide)
        got = dot(pieces, lane1h[:, lanes], NN)
        own_c, rank_c = chunk_key(c, width)
        key_c = (own_c >> gy_bits) * 2 + (rank_c >> 1)
        half = sub_of(wide) >> 2
        picked = jnp.zeros((8, wide), jnp.float32)
        for r in range(16):
            tile = got[8 * r : 8 * r + 8]
            for i in range(1, PIECES):
                tile = tile + got[128 * i + 8 * r : 128 * i + 8 * r + 8]
            picked = picked + jnp.where(key_c == half + 2 * r, tile, 0.0)
        picked = (picked + pltpu.roll(picked, 4, 0)) * weights(c, width)
        _, row_c = row_of(c, width)
        hit = (iota((128, wide), 0) >> 3) == row_c
        parts = [
            jnp.where(hit, jnp.concatenate([part.astype(jnp.float32)] * 16, axis=0), 0.0).astype(jnp.bfloat16)
            for part in split(picked)
        ]
        acc = acc + dot(jnp.concatenate(parts, axis=0), win[:, lanes], NT)
    total = acc[0:128]
    for i in range(1, PIECES):
        total = total + acc[128 * i : 128 * i + 128]
    load[...] = total

    def put_strip2(side, u, value):
        strip2[side] = value

    pack(lambda i: load[8 * i : 8 * i + 8, :], 16, put_strip2)
    copies = halo_copies(load, xr2, strip2, yr2, h2send, h2recv)
    ext[...] = jnp.zeros_like(ext)
    for copy in copies:
        copy.wait()
    for g in range(3):
        both = comb(yr2, g, 0)
        for k in range(16):
            halo2[g, pl.ds(8 * k, 8), :] = pltpu.roll(both, (124 - 8 * k) % 128, 1)
    sources = ((xr2.at[0], first_x), (load, None), (xr2.at[1], last_x))
    for f in range(2):
        for t in range(STEPS):
            for z in range(4):
                rows = pl.ds(32 * z + 4 * f + t, 4, stride=8)
                for g, (ref, drop) in enumerate(sources):
                    part = ref[rows, :]
                    if drop is not None:
                        part = jnp.where(drop, 0.0, part)
                    exl[2 * t + f, 16 * z + 4 * g : 16 * z + 4 * g + 4, 0:128] = part
                    exl[2 * t + f, 16 * z + 4 * g : 16 * z + 4 * g + 4, 128:256] = halo2[g, rows, :]

    lam_grad = jnp.zeros((16, 128), jnp.float32)
    mu_grad = jnp.zeros((16, 128), jnp.float32)
    for k in range(STEPS):
        t = STEPS - 1 - k
        for f in range(2):
            ext[3 + f] = ext[3 + f] + exl[2 * t + f]

        def emit(z, e):
            for i in range(6):
                ad[i, pl.ds(4 * z, 4), :] = e[i]

        time_step(ext, mats, emit)
        fwd = [es[6 * t + i] for i in range(6)]
        adj = [ad[i] for i in range(6)]
        prod = [a * b for a, b in zip(fwd, adj)]
        lam_grad = lam_grad + (fwd[0] + fwd[1] + fwd[2]) * (adj[0] + adj[1] + adj[2])
        mu_grad = mu_grad + (2.0 * (prod[0] + prod[1] + prod[2]) + prod[3] + prod[4] + prod[5])
    grad_out[0:16, :] = lam_grad
    grad_out[16:32, :] = mu_grad


def shards(
    initial_state,
    lame_lambda,
    shear_modulus,
    buoyancy,
    source_cells,
    source_wavelet,
    segment_start,
    segment_weight,
    partial_owner,
    partial_channel,
    observed_data,
):
    ngx, ngy = lax.axis_size("gx"), lax.axis_size("gy")
    npart = segment_start.shape[0]
    nsrc = source_cells.shape[0]
    f32, bf16 = jnp.float32, jnp.bfloat16
    vmem = pl.BlockSpec(memory_space=pltpu.VMEM)
    dma = pltpu.SemaphoreType.DMA
    scratch = [
        pltpu.VMEM((16 * NF, 128), f32),
        pltpu.VMEM((2, 16 * NF, 128), f32),
        pltpu.VMEM((2, 16, 128), f32),
        pltpu.VMEM((3, 2, 16, 128), f32),
        pltpu.VMEM((9, 64, 256), f32),
        pltpu.VMEM((3, 64, 256), f32),
        pltpu.VMEM((48, 128), f32),
        pltpu.VMEM((6 * STEPS, 16, 128), f32),
        pltpu.VMEM((6, 16, 128), f32),
        pltpu.VMEM((128, 128), f32),
        pltpu.VMEM((npart // 128, 128, 128), f32),
        pltpu.VMEM((npart // 128, 128), f32),
        pltpu.VMEM((128, npart), bf16),
        pltpu.VMEM((128, npart), bf16),
        pltpu.VMEM((32, 128), f32),
        pltpu.VMEM((16, 8, 128), f32),
        pltpu.VMEM((16, 8, 128), f32),
        pltpu.VMEM((64, 2, 128), f32),
        pltpu.VMEM((64, 2, 128), f32),
        pltpu.VMEM((128, 128), f32),
        pltpu.VMEM((128, 4096), bf16),
        pltpu.VMEM((16, 256), jnp.int32),
        pltpu.VMEM((64, 2, 128), f32),
        pltpu.VMEM((64, 2, 128), f32),
        pltpu.VMEM((16, 8, 128), f32),
        pltpu.VMEM((16, 8, 128), f32),
        pltpu.VMEM((128, 128), f32),
        pltpu.VMEM((2, 128, 128), f32),
        pltpu.VMEM((2, 8, 128), f32),
        pltpu.VMEM((3, 2, 8, 128), f32),
        pltpu.VMEM((3, 128, 128), f32),
        pltpu.VMEM((2 * STEPS, 64, 256), f32),
        dma((8,)),
        dma((8,)),
        dma((8,)),
        dma((8,)),
        dma((4,)),
        dma((4,)),
    ]
    residuals, gradients = pl.pallas_call(
        functools.partial(kernel, ngx, ngy, npart),
        out_shape=(
            jax.ShapeDtypeStruct(observed_data.shape, f32),
            jax.ShapeDtypeStruct((32, 128), f32),
        ),
        in_specs=[vmem] * 11,
        out_specs=(vmem, vmem),
        scratch_shapes=scratch,
        compiler_params=pltpu.CompilerParams(collective_id=0, has_side_effects=True),
        name="window",
    )(
        initial_state.reshape(144, 128),
        lame_lambda.reshape(16, 128),
        shear_modulus.reshape(16, 128),
        buoyancy.reshape(16, 128),
        source_cells.reshape(1, nsrc),
        source_wavelet,
        segment_start.reshape(-1, 128),
        segment_weight,
        partial_owner.reshape(-1, 128),
        partial_channel.reshape(-1, 128),
        observed_data,
    )
    return residuals, gradients.reshape(2, 4, 4, 128)


def solution(mesh):
    in_specs = (
        P(None, None, "gx", "gy"),
        P(None, "gx", "gy"),
        P(None, "gx", "gy"),
        P(None, "gx", "gy"),
        P(("gx", "gy")),
        P(None, ("gx", "gy")),
        P(("gx", "gy")),
        P(None, ("gx", "gy")),
        P(("gx", "gy"), None),
        P(("gx", "gy")),
        P(None, ("gx", "gy")),
    )
    out_specs = (P(None, ("gx", "gy")), P(None, None, "gx", "gy"))
    return jax.shard_map(shards, mesh=mesh, in_specs=in_specs, out_specs=out_specs, check_vma=False)
```

```python
import functools

import jax
import jax.numpy as jnp
from jax import lax
from jax.experimental import pallas as pl
from jax.experimental.pallas import tpu as pltpu
from jax.sharding import PartitionSpec as P

GAUGE = 8
DT = 0.25
PIECES = 3
STEPS = 3
NF = 14
MESH = pl.DeviceIdType.MESH
NT = (((1,), (1,)), ((), ()))
NN = (((1,), (0,)), ((), ()))


def iota(shape, dim):
    return lax.broadcasted_iota(jnp.int32, shape, dim)


def split(x):
    parts = []
    for _ in range(PIECES):
        part = x.astype(jnp.bfloat16)
        parts.append(part)
        x = x - part.astype(jnp.float32)
    return parts


def dot(a, b, dims):
    return lax.dot_general(a, b, dims, preferred_element_type=jnp.float32)


def dot_split(x, b, dims):
    parts = split(x)
    rows = x.shape[0]
    stacked = dot(jnp.concatenate(parts, axis=0), b, dims)
    total = stacked[:rows]
    for i in range(1, PIECES):
        total = total + stacked[i * rows : (i + 1) * rows]
    return total


def ones_where(mask):
    return jnp.where(mask, 1.0, 0.0).astype(jnp.bfloat16)


def ahead(f, axis):
    return pltpu.roll(f, f.shape[axis] - 1, axis) - f


def behind(f, axis):
    return f - pltpu.roll(f, 1, axis)


def time_step(ext, mats, emit):
    def plane(ref, f, z):
        return ref[f, pl.ds(16 * z, 16), :]

    def ahead_z(f, z):
        return (plane(ext, f, z + 1) if z < 3 else 0.0) - plane(ext, f, z)

    def behind_z(f, z):
        here = plane(ext, f, z)
        return here - plane(ext, f, z - 1) if z > 0 else here

    for z in range(4):
        scale = DT * plane(mats, 0, z)
        sxy, sxz, syz = plane(ext, 6, z), plane(ext, 7, z), plane(ext, 8, z)
        ax = ahead(plane(ext, 3, z), 0) + behind(sxy, 1) + behind_z(7, z)
        ay = behind(sxy, 0) + ahead(plane(ext, 4, z), 1) + behind_z(8, z)
        az = behind(sxz, 0) + behind(syz, 1) + ahead_z(5, z)
        for f, a in enumerate((ax, ay, az)):
            ext[f, pl.ds(16 * z, 16), :] = plane(ext, f, z) + scale * a
    for z in range(4):
        vx, vy, vz = plane(ext, 0, z), plane(ext, 1, z), plane(ext, 2, z)
        exx = behind(vx, 0)
        eyy = behind(vy, 1)
        ezz = behind_z(2, z)
        exy = ahead(vx, 1) + ahead(vy, 0)
        exz = ahead_z(0, z) + ahead(vz, 0)
        eyz = ahead_z(1, z) + ahead(vz, 1)
        emit(z, [e[4:8, 0:128] for e in (exx, eyy, ezz, exy, exz, eyz)])
        lam, mu = plane(mats, 1, z), plane(mats, 2, z)
        dil = lam * (exx + eyy + ezz)
        for f, e in ((3, exx), (4, eyy), (5, ezz)):
            ext[f, pl.ds(16 * z, 16), :] = plane(ext, f, z) + DT * (dil + 2.0 * mu * e)
        for f, e in ((6, exy), (7, exz), (8, eyz)):
            ext[f, pl.ds(16 * z, 16), :] = plane(ext, f, z) + DT * mu * e


def kernel(
    ngx,
    ngy,
    npart,
    state_in,
    lam_in,
    mu_in,
    buoy_in,
    scell_in,
    swave_in,
    start_in,
    weight_in,
    owner_in,
    chan_in,
    obs_in,
    res_out,
    grad_out,
    scell,
    swave,
    start,
    weight,
    owner,
    chan,
    obs,
    res,
    grad,
    own,
    xr,
    strip,
    yr,
    ext,
    mats,
    srcs,
    es,
    ad,
    glhs,
    colb,
    rank,
    win,
    lane1h,
    obs32,
    sa,
    ra,
    sx,
    rx,
    arr,
    chan1h,
    hirow,
    sx2,
    rx2,
    sa2,
    ra2,
    load,
    xr2,
    strip2,
    yr2,
    halo2,
    exl,
    hsend,
    hrecv,
    h2send,
    h2recv,
    esend,
    erecv,
    isem,
    osem,
    ready,
):
    gx, gy = lax.axis_index("gx"), lax.axis_index("gy")
    nchunk = npart // 128
    gy_bits = ngy.bit_length() - 1
    y_bits = gy_bits // 2
    ny = 1 << y_bits
    nx = ngy // ny
    right_x, left_x = lax.rem(gx + 1, ngx), lax.rem(gx + ngx - 1, ngx)
    right_y, left_y = lax.rem(gy + 1, ngy), lax.rem(gy + ngy - 1, ngy)
    first_x, last_x = gx == 0, gx == ngx - 1
    first_y, last_y = gy == 0, gy == ngy - 1

    if ngx < 16 or ngy < 64:
        for ref in (ra, rx, rx2, ra2):
            ref[...] = jnp.zeros_like(ref)

    barrier = pltpu.get_barrier_semaphore()

    def greet(x, y):
        pl.semaphore_signal(barrier, inc=1, device_id={"gx": x, "gy": y}, device_id_type=MESH)

    reads = [
        pltpu.make_async_copy(src, dst, isem.at[i])
        for i, (src, dst) in enumerate(
            (
                (state_in, own.at[pl.ds(0, 144)]),
                (scell_in, scell),
                (swave_in, swave),
                (buoy_in, own.at[pl.ds(144, 16)]),
                (lam_in, own.at[pl.ds(160, 16)]),
                (mu_in, own.at[pl.ds(176, 16)]),
                (owner_in, owner),
                (start_in, start),
                (chan_in, chan),
                (weight_in, weight),
                (obs_in, obs),
            )
        )
    ]
    for read in reads:
        read.start()

    def far_first(count):
        return sorted(range(1, count), key=lambda i: -min(i, count - i))

    def peer_z(i):
        return lax.rem(gx + i, ngx), gy

    def peer_x(i):
        return gx, lax.rem((gy >> y_bits) + i, nx) * ny + (gy & (ny - 1))

    def peer_y(i):
        return gx, (gy & ~(ny - 1)) + lax.rem((gy & (ny - 1)) + i, ny)

    greeted = [peer_z(i) for i in far_first(ngx)] + [peer_x(i) for i in far_first(nx)] + [peer_y(i) for i in far_first(ny)]
    greeted += [(x, y) for y in (left_y, right_y) for x in (gx, left_x, right_x)]
    for x, y in greeted:
        greet(x, y)

    mats[...] = jnp.zeros_like(mats)
    ext[...] = jnp.zeros_like(ext)
    exl[...] = jnp.zeros_like(exl)
    glhs[...] = jnp.zeros_like(glhs)
    obs32[...] = jnp.zeros_like(obs32)
    for read in reads[:6]:
        read.wait()

    cell = scell[...]
    nsrc = cell.shape[1]
    key = iota((48, nsrc), 0)
    wave = jnp.concatenate([jnp.broadcast_to(swave[t : t + 1, :], (16, nsrc)) for t in range(STEPS)], axis=0)
    lhs = jnp.where((key & 15) == (cell >> 7), wave, 0.0)
    srcs[...] = dot_split(lhs, ones_where(iota((128, nsrc), 0) == (cell & 127)), NT)
    for f in (3, 4, 5):
        own[16 * f : 16 * f + 16, :] = own[16 * f : 16 * f + 16, :] + srcs[0:16, :]
    own[192:224, :] = srcs[16:48, :]

    lane = iota((8, 128), 1)
    sub = iota((8, 128), 0)
    low4 = (lane & 7) < 4

    def pack(tile_of, groups, put):
        for u in range(-(-groups // 16)):
            acc = [jnp.zeros((8, 128), jnp.float32)] * 2
            for k in range(min(16, groups - 16 * u)):
                tile = tile_of(16 * u + k)
                here = (lane >> 3) == k
                acc[0] = jnp.where(here, pltpu.roll(tile, (8 * k - 124) % 128, 1), acc[0])
                acc[1] = jnp.where(here, pltpu.roll(tile, (8 * k + 4) % 128, 1), acc[1])
            for side in range(2):
                put(side, u, acc[side])

    def put_strip(side, u, value):
        strip[side, pl.ds(8 * u, 8), :] = value

    pack(lambda i: own[8 * i : 8 * i + 8, :], 2 * NF, put_strip)

    pl.semaphore_wait(barrier, len(greeted))
    for i in far_first(nx):
        x, y = peer_x(i)
        pl.semaphore_signal(ready, inc=1, device_id={"gx": x, "gy": y}, device_id_type=MESH)

    def halo_copies(rows, rows_to, strips, strips_to, send, recv):
        plan = [
            (rows, rows_to.at[0], right_x, gy),
            (rows, rows_to.at[1], left_x, gy),
            (strips.at[0], strips_to.at[1, 0], gx, right_y),
            (strips.at[1], strips_to.at[1, 1], gx, left_y),
            (strips.at[0], strips_to.at[0, 0], right_x, right_y),
            (strips.at[1], strips_to.at[0, 1], right_x, left_y),
            (strips.at[0], strips_to.at[2, 0], left_x, right_y),
            (strips.at[1], strips_to.at[2, 1], left_x, left_y),
        ]
        copies = [
            pltpu.make_async_remote_copy(
                src_ref=src,
                dst_ref=dst,
                send_sem=send.at[i],
                recv_sem=recv.at[i],
                device_id={"gx": x, "gy": y},
                device_id_type=MESH,
            )
            for i, (src, dst, x, y) in enumerate(plan)
        ]
        for copy in copies:
            copy.start()
        return copies

    copies = halo_copies(own, xr, strip, yr, hsend, hrecv)
    for read in reads[6:]:
        read.wait()

    ownf = owner[...].astype(jnp.float32)
    cols = jnp.concatenate([ownf, jnp.zeros((128 - nchunk, 128), jnp.float32)], axis=0).T
    for c in range(nchunk):
        colb[c] = jnp.broadcast_to(cols[:, c : c + 1], (128, 128))
    earlier = iota((128, 128), 0) < iota((128, 128), 1)

    @pl.loop(0, nchunk)
    def _(c):
        row = jnp.broadcast_to(owner[pl.ds(c, 1), :].astype(jnp.float32), (128, 128))
        same = jnp.where((colb[c] == row) & earlier, 1.0, 0.0)

        def more(q, count):
            hit = jnp.where(colb[q] == row, 1.0, 0.0)
            return count + hit.reshape(16, 8, 128).sum(axis=0)

        count = lax.fori_loop(0, c, more, same.reshape(16, 8, 128).sum(axis=0))
        rank[pl.ds(c, 1), :] = jnp.sum(count, axis=0, keepdims=True)

    for i in range(8):
        obs32[4 * i : 4 * i + 3, :] = obs[:, 128 * i : 128 * i + 128]


    def chunk_key(c, width):
        own_c = jnp.concatenate([owner[c + i : c + i + 1, :] for i in range(width)], axis=1)
        rank_c = jnp.concatenate([rank[c + i : c + i + 1, :] for i in range(width)], axis=1).astype(jnp.int32)
        return own_c, rank_c

    def row_of(c, width):
        start_c = jnp.concatenate([start[c + i : c + i + 1, :] for i in range(width)], axis=1)
        row_c = (start_c * 8666) >> 20
        return start_c, row_c

    for c in range(nchunk):
        start_c, row_c = row_of(c, 1)
        ahead_c = iota((128, 128), 0) - (start_c - 121 * row_c)
        win[:, 128 * c : 128 * c + 128] = ones_where((ahead_c >= 0) & (ahead_c < GAUGE))
        own_c, rank_c = chunk_key(c, 1)
        lane_c = (own_c & (ngy - 1)) * 2 + (rank_c & 1)
        lane1h[:, 128 * c : 128 * c + 128] = ones_where(iota((128, 128), 0) == lane_c)

    def place_rows(g, rows_ref, drop):
        for f in range(NF):
            for z in range(4):
                part = rows_ref[16 * f + 4 * z : 16 * f + 4 * z + 4, :]
                if drop is not None:
                    part = jnp.where(drop, 0.0, part)
                put_ext(f, slice(16 * z + 4 * g, 16 * z + 4 * g + 4), slice(0, 128), part)

    def put_ext(f, rows, lanes, value):
        if f < 9:
            ext[f, rows, lanes] = value
        elif f < 12:
            mats[f - 9, rows, lanes] = value
        else:
            exl[f - 12, rows, lanes] = value

    def comb(strips, g, u):
        low = jnp.where(first_y, 0.0, strips[g, 0, pl.ds(8 * u, 8), :])
        high = jnp.where(last_y, 0.0, strips[g, 1, pl.ds(8 * u, 8), :])
        both = jnp.where(low4, low, high)
        if g == 0:
            both = jnp.where(first_x, 0.0, both)
        if g == 2:
            both = jnp.where(last_x, 0.0, both)
        return both

    place_rows(1, own, None)
    for copy in copies:
        copy.wait()
    place_rows(0, xr.at[0], first_x)
    place_rows(2, xr.at[1], last_x)
    for g in range(3):
        for u in range(2):
            both = comb(yr, g, u)
            for k in range(min(16, 2 * NF - 16 * u)):
                f, h = divmod(16 * u + k, 2)
                tile = pltpu.roll(both, (124 - 8 * k) % 128, 1)
                for i in range(2):
                    z = 2 * h + i
                    put_ext(f, slice(16 * z + 4 * g, 16 * z + 4 * g + 4), slice(128, 256), tile[4 * i : 4 * i + 4, :])

    for t in range(STEPS):
        if t > 0:
            for f in (3, 4, 5):
                ext[f] = ext[f] + exl[t - 1]

        def emit(z, e, t=t):
            for i in range(6):
                es[6 * t + i, pl.ds(4 * z, 4), :] = e[i]
            for f in range(2):
                glhs[pl.ds(32 * z + 4 * f + t, 4, stride=8), :] = e[f]

        time_step(ext, mats, emit)

    def sub_of(width):
        return iota((8, width), 0)

    def weights(c, width):
        both = weight[:, 128 * c : 128 * (c + width)]
        return jnp.where(sub_of(128 * width) < 4, both[0:1, :], both[1:2, :])

    width = 2 if nchunk % 2 == 0 else 1
    wide = 128 * width
    gpieces = jnp.concatenate(split(glhs[...]), axis=0)
    acc = jnp.zeros((PIECES * 128, 128), jnp.float32)
    for c in range(0, nchunk, width):
        lanes = slice(128 * c, 128 * c + wide)
        _, row_c = row_of(c, width)
        got = dot(gpieces, win[:, lanes], NN)
        picked = jnp.zeros((8, wide), jnp.float32)
        for r in range(16):
            tile = got[8 * r : 8 * r + 8]
            for i in range(1, PIECES):
                tile = tile + got[128 * i + 8 * r : 128 * i + 8 * r + 8]
            picked = picked + jnp.where(row_c == r, tile, 0.0)
        picked = picked * weights(c, width)
        picked = picked + pltpu.roll(picked, 4, 0)
        chan_c = jnp.concatenate([chan[c + i : c + i + 1, :] for i in range(width)], axis=1)
        picked = jnp.where((sub_of(wide) & 3) == 3, chan_c.astype(jnp.float32), picked)
        own_c, rank_c = chunk_key(c, width)
        key_c = (own_c >> gy_bits) * 2 + (rank_c >> 1)
        hit = (iota((128, wide), 0) >> 2) == key_c
        parts = [
            jnp.where(hit, jnp.concatenate([part.astype(jnp.float32)] * 16, axis=0), 0.0).astype(jnp.bfloat16)
            for part in split(picked)
        ]
        acc = acc + dot(jnp.concatenate(parts, axis=0), lane1h[:, lanes], NT)
    total = acc[0:128]
    for i in range(1, PIECES):
        total = total + acc[128 * i : 128 * i + 128]
    sa[...] = total.reshape(16, 8, 128)

    def exchange(stage, peers, me, src, dst):
        send, recv = esend.at[stage], erecv.at[stage]
        for place, x, y in peers:
            pltpu.make_async_remote_copy(
                src_ref=src.at[place],
                dst_ref=dst.at[me],
                send_sem=send,
                recv_sem=recv,
                device_id={"gx": x, "gy": y},
                device_id_type=MESH,
            ).start()
        pltpu.make_async_copy(src.at[me], dst.at[me], recv).start()
        whole, less = dst.at[pl.ds(0, len(peers) + 1)], src.at[pl.ds(0, len(peers))]
        pltpu.make_async_copy(whole, whole, recv).wait()
        pltpu.make_async_copy(less, less, send).wait()

    z_peers = [(lax.rem(gx + i, ngx), lax.rem(gx + i, ngx), gy) for i in far_first(ngx)]
    xs = [lax.rem((gy >> y_bits) + i, nx) * ny for i in range(nx)]
    ys = [lax.rem((gy & (ny - 1)) + i, ny) for i in range(ny)]
    offsets = [(i, j) for i in range(nx) for j in range(ny) if i or j]
    offsets.sort(key=lambda o: -min(o[0], nx - o[0]) - min(o[1], ny - o[1]))
    xy_peers = [(xs[i] + ys[j], gx, xs[i] + ys[j]) for i, j in offsets]

    exchange(0, z_peers, gx, sa, ra)
    sx[...] = ra[...].reshape(128, 128).T.reshape(64, 2, 128)
    pl.semaphore_wait(ready, nx - 1)
    exchange(1, xy_peers, gy, sx, rx)
    arr[...] = rx[...].reshape(128, 128).T

    acc = jnp.zeros((PIECES * 32, 128), jnp.float32)
    sub256 = sub_of(256) >> 2
    for d in range(16):
        tile = arr[8 * d : 8 * d + 8, :]
        turned = pltpu.roll(tile, 4, 0)
        both = jnp.concatenate([jnp.where(sub < 4, tile, turned), jnp.where(sub < 4, turned, tile)], axis=1)
        ids = both[3:4, :].astype(jnp.int32)
        onehot = ones_where(iota((128, 256), 0) == (ids & 127))
        chan1h[:, 256 * d : 256 * d + 256] = onehot
        hi = ids >> 7
        hirow[d : d + 1, :] = hi
        parts = []
        for part in split(both):
            part = part.astype(jnp.float32)
            for j in range(4):
                parts.append(jnp.where(hi == sub256 + 2 * j, part, 0.0).astype(jnp.bfloat16))
        acc = acc + dot(jnp.concatenate(parts, axis=0), onehot, NT)
    sums = acc[0:32]
    for i in range(1, PIECES):
        sums = sums + acc[32 * i : 32 * i + 32]
    sums = jnp.where((iota((32, 128), 0) & 3) == 3, 0.0, sums - obs32[...])
    for i in range(8):
        res[:, 128 * i : 128 * i + 128] = sums[4 * i : 4 * i + 3, :]
    put_res = pltpu.make_async_copy(res, res_out, osem.at[0])
    put_res.start()

    pieces = jnp.concatenate(split(sums), axis=0)
    for d in range(16):
        got = dot(pieces, chan1h[:, 256 * d : 256 * d + 256], NN)
        hi = hirow[d : d + 1, :]
        picked = jnp.zeros((8, 256), jnp.float32)
        for j in range(4):
            tile = got[8 * j : 8 * j + 8]
            for i in range(1, PIECES):
                tile = tile + got[32 * i + 8 * j : 32 * i + 8 * j + 8]
            picked = picked + jnp.where(hi == sub256 + 2 * j, tile, 0.0)
        picked = picked + pltpu.roll(picked, 4, 0)
        arr[8 * d : 8 * d + 8, :] = jnp.where(sub < 4, picked[:, 0:128], picked[:, 128:256])
    sx2[...] = arr[...].T.reshape(64, 2, 128)
    exchange(2, xy_peers, gy, sx2, rx2)
    sa2[...] = rx2[...].reshape(128, 128).T.reshape(16, 8, 128)
    exchange(3, z_peers, gx, sa2, ra2)

    pieces = jnp.concatenate(split(ra2[...].reshape(128, 128)), axis=0)
    acc = jnp.zeros((PIECES * 128, 128), jnp.float32)
    for c in range(0, nchunk, width):
        lanes = slice(128 * c, 128 * c + wide)
        got = dot(pieces, lane1h[:, lanes], NN)
        own_c, rank_c = chunk_key(c, width)
        key_c = (own_c >> gy_bits) * 2 + (rank_c >> 1)
        half = sub_of(wide) >> 2
        picked = jnp.zeros((8, wide), jnp.float32)
        for r in range(16):
            tile = got[8 * r : 8 * r + 8]
            for i in range(1, PIECES):
                tile = tile + got[128 * i + 8 * r : 128 * i + 8 * r + 8]
            picked = picked + jnp.where(key_c == half + 2 * r, tile, 0.0)
        picked = (picked + pltpu.roll(picked, 4, 0)) * weights(c, width)
        _, row_c = row_of(c, width)
        hit = (iota((128, wide), 0) >> 3) == row_c
        parts = [
            jnp.where(hit, jnp.concatenate([part.astype(jnp.float32)] * 16, axis=0), 0.0).astype(jnp.bfloat16)
            for part in split(picked)
        ]
        acc = acc + dot(jnp.concatenate(parts, axis=0), win[:, lanes], NT)
    total = acc[0:128]
    for i in range(1, PIECES):
        total = total + acc[128 * i : 128 * i + 128]
    load[...] = total

    def put_strip2(side, u, value):
        strip2[side] = value

    pack(lambda i: load[8 * i : 8 * i + 8, :], 16, put_strip2)
    copies = halo_copies(load, xr2, strip2, yr2, h2send, h2recv)
    ext[...] = jnp.zeros_like(ext)
    for copy in copies:
        copy.wait()
    for g in range(3):
        both = comb(yr2, g, 0)
        for k in range(16):
            halo2[g, pl.ds(8 * k, 8), :] = pltpu.roll(both, (124 - 8 * k) % 128, 1)
    sources = ((xr2.at[0], first_x), (load, None), (xr2.at[1], last_x))
    for f in range(2):
        for t in range(STEPS):
            for z in range(4):
                rows = pl.ds(32 * z + 4 * f + t, 4, stride=8)
                for g, (ref, drop) in enumerate(sources):
                    part = ref[rows, :]
                    if drop is not None:
                        part = jnp.where(drop, 0.0, part)
                    exl[2 * t + f, 16 * z + 4 * g : 16 * z + 4 * g + 4, 0:128] = part
                    exl[2 * t + f, 16 * z + 4 * g : 16 * z + 4 * g + 4, 128:256] = halo2[g, rows, :]

    lam_grad = jnp.zeros((16, 128), jnp.float32)
    mu_grad = jnp.zeros((16, 128), jnp.float32)
    for k in range(STEPS):
        t = STEPS - 1 - k
        for f in range(2):
            ext[3 + f] = ext[3 + f] + exl[2 * t + f]

        def emit(z, e):
            for i in range(6):
                ad[i, pl.ds(4 * z, 4), :] = e[i]

        time_step(ext, mats, emit)
        fwd = [es[6 * t + i] for i in range(6)]
        adj = [ad[i] for i in range(6)]
        prod = [a * b for a, b in zip(fwd, adj)]
        lam_grad = lam_grad + (fwd[0] + fwd[1] + fwd[2]) * (adj[0] + adj[1] + adj[2])
        mu_grad = mu_grad + (2.0 * (prod[0] + prod[1] + prod[2]) + prod[3] + prod[4] + prod[5])
    grad[0:16, :] = lam_grad
    grad[16:32, :] = mu_grad
    put_grad = pltpu.make_async_copy(grad, grad_out, osem.at[1])
    put_grad.start()
    put_res.wait()
    put_grad.wait()


def shards(
    initial_state,
    lame_lambda,
    shear_modulus,
    buoyancy,
    source_cells,
    source_wavelet,
    segment_start,
    segment_weight,
    partial_owner,
    partial_channel,
    observed_data,
):
    ngx, ngy = lax.axis_size("gx"), lax.axis_size("gy")
    npart = segment_start.shape[0]
    nsrc = source_cells.shape[0]
    f32, bf16 = jnp.float32, jnp.bfloat16
    anywhere = pl.BlockSpec(memory_space=pl.ANY)
    dma = pltpu.SemaphoreType.DMA
    scratch = [
        pltpu.VMEM((1, nsrc), jnp.int32),
        pltpu.VMEM((STEPS, nsrc), f32),
        pltpu.VMEM((npart // 128, 128), jnp.int32),
        pltpu.VMEM((2, npart), f32),
        pltpu.VMEM((npart // 128, 128), jnp.int32),
        pltpu.VMEM((npart // 128, 128), jnp.int32),
        pltpu.VMEM(observed_data.shape, f32),
        pltpu.VMEM(observed_data.shape, f32),
        pltpu.VMEM((32, 128), f32),
        pltpu.VMEM((16 * NF, 128), f32),
        pltpu.VMEM((2, 16 * NF, 128), f32),
        pltpu.VMEM((2, 16, 128), f32),
        pltpu.VMEM((3, 2, 16, 128), f32),
        pltpu.VMEM((9, 64, 256), f32),
        pltpu.VMEM((3, 64, 256), f32),
        pltpu.VMEM((48, 128), f32),
        pltpu.VMEM((6 * STEPS, 16, 128), f32),
        pltpu.VMEM((6, 16, 128), f32),
        pltpu.VMEM((128, 128), f32),
        pltpu.VMEM((npart // 128, 128, 128), f32),
        pltpu.VMEM((npart // 128, 128), f32),
        pltpu.VMEM((128, npart), bf16),
        pltpu.VMEM((128, npart), bf16),
        pltpu.VMEM((32, 128), f32),
        pltpu.VMEM((16, 8, 128), f32),
        pltpu.VMEM((16, 8, 128), f32),
        pltpu.VMEM((64, 2, 128), f32),
        pltpu.VMEM((64, 2, 128), f32),
        pltpu.VMEM((128, 128), f32),
        pltpu.VMEM((128, 4096), bf16),
        pltpu.VMEM((16, 256), jnp.int32),
        pltpu.VMEM((64, 2, 128), f32),
        pltpu.VMEM((64, 2, 128), f32),
        pltpu.VMEM((16, 8, 128), f32),
        pltpu.VMEM((16, 8, 128), f32),
        pltpu.VMEM((128, 128), f32),
        pltpu.VMEM((2, 128, 128), f32),
        pltpu.VMEM((2, 8, 128), f32),
        pltpu.VMEM((3, 2, 8, 128), f32),
        pltpu.VMEM((3, 128, 128), f32),
        pltpu.VMEM((2 * STEPS, 64, 256), f32),
        dma((8,)),
        dma((8,)),
        dma((8,)),
        dma((8,)),
        dma((4,)),
        dma((4,)),
        dma((11,)),
        dma((2,)),
        pltpu.SemaphoreType.REGULAR,
    ]
    residuals, gradients = pl.pallas_call(
        functools.partial(kernel, ngx, ngy, npart),
        out_shape=(
            jax.ShapeDtypeStruct(observed_data.shape, f32),
            jax.ShapeDtypeStruct((32, 128), f32),
        ),
        in_specs=[anywhere] * 11,
        out_specs=(anywhere, anywhere),
        scratch_shapes=scratch,
        compiler_params=pltpu.CompilerParams(collective_id=0, has_side_effects=True),
        name="window",
    )(
        initial_state.reshape(144, 128),
        lame_lambda.reshape(16, 128),
        shear_modulus.reshape(16, 128),
        buoyancy.reshape(16, 128),
        source_cells.reshape(1, nsrc),
        source_wavelet,
        segment_start.reshape(-1, 128),
        segment_weight,
        partial_owner.reshape(-1, 128),
        partial_channel.reshape(-1, 128),
        observed_data,
    )
    return residuals, gradients.reshape(2, 4, 4, 128)


def solution(mesh):
    in_specs = (
        P(None, None, "gx", "gy"),
        P(None, "gx", "gy"),
        P(None, "gx", "gy"),
        P(None, "gx", "gy"),
        P(("gx", "gy")),
        P(None, ("gx", "gy")),
        P(("gx", "gy")),
        P(None, ("gx", "gy")),
        P(("gx", "gy"), None),
        P(("gx", "gy")),
        P(None, ("gx", "gy")),
    )
    out_specs = (P(None, ("gx", "gy")), P(None, None, "gx", "gy"))
    return jax.shard_map(shards, mesh=mesh, in_specs=in_specs, out_specs=out_specs, check_vma=False)
```

```python
import functools

import jax
import jax.numpy as jnp
from jax import lax
from jax.experimental import pallas as pl
from jax.experimental.pallas import tpu as pltpu
from jax.sharding import PartitionSpec as P

GAUGE = 8
DT = 0.25
PIECES = 3
STEPS = 3
NF = 14
MESH = pl.DeviceIdType.MESH
NT = (((1,), (1,)), ((), ()))
NN = (((1,), (0,)), ((), ()))


def iota(shape, dim):
    return lax.broadcasted_iota(jnp.int32, shape, dim)


def split(x):
    parts = []
    for _ in range(PIECES):
        part = x.astype(jnp.bfloat16)
        parts.append(part)
        x = x - part.astype(jnp.float32)
    return parts


def dot(a, b, dims):
    return lax.dot_general(a, b, dims, preferred_element_type=jnp.float32)


def dot_split(x, b, dims):
    parts = split(x)
    rows = x.shape[0]
    stacked = dot(jnp.concatenate(parts, axis=0), b, dims)
    total = stacked[:rows]
    for i in range(1, PIECES):
        total = total + stacked[i * rows : (i + 1) * rows]
    return total


def ones_where(mask):
    return jnp.where(mask, 1.0, 0.0).astype(jnp.bfloat16)


def narrow(x):
    return x.astype(jnp.float32).astype(jnp.bfloat16)


def spread_rows(x, key_rows, key, copies):
    hit = key_rows == narrow(key)
    zero = jnp.zeros(hit.shape, jnp.bfloat16)
    pieces = split(jnp.concatenate([x, x], axis=0))
    return jnp.concatenate(
        [jnp.where(hit, jnp.concatenate([piece] * copies, axis=0), zero) for piece in pieces], axis=0
    )


def ahead(f, axis):
    return pltpu.roll(f, f.shape[axis] - 1, axis) - f


def behind(f, axis):
    return f - pltpu.roll(f, 1, axis)


def time_step(ext, mats, emit):
    def plane(ref, f, z):
        return ref[f, pl.ds(16 * z, 16), :]

    def ahead_z(f, z):
        return (plane(ext, f, z + 1) if z < 3 else 0.0) - plane(ext, f, z)

    def behind_z(f, z):
        here = plane(ext, f, z)
        return here - plane(ext, f, z - 1) if z > 0 else here

    for z in range(4):
        scale = DT * plane(mats, 0, z)
        sxy, sxz, syz = plane(ext, 6, z), plane(ext, 7, z), plane(ext, 8, z)
        ax = ahead(plane(ext, 3, z), 0) + behind(sxy, 1) + behind_z(7, z)
        ay = behind(sxy, 0) + ahead(plane(ext, 4, z), 1) + behind_z(8, z)
        az = behind(sxz, 0) + behind(syz, 1) + ahead_z(5, z)
        for f, a in enumerate((ax, ay, az)):
            ext[f, pl.ds(16 * z, 16), :] = plane(ext, f, z) + scale * a
    for z in range(4):
        vx, vy, vz = plane(ext, 0, z), plane(ext, 1, z), plane(ext, 2, z)
        exx = behind(vx, 0)
        eyy = behind(vy, 1)
        ezz = behind_z(2, z)
        exy = ahead(vx, 1) + ahead(vy, 0)
        exz = ahead_z(0, z) + ahead(vz, 0)
        eyz = ahead_z(1, z) + ahead(vz, 1)
        emit(z, [e[4:8, 0:128] for e in (exx, eyy, ezz, exy, exz, eyz)])
        lam, mu = plane(mats, 1, z), plane(mats, 2, z)
        dil = lam * (exx + eyy + ezz)
        for f, e in ((3, exx), (4, eyy), (5, ezz)):
            ext[f, pl.ds(16 * z, 16), :] = plane(ext, f, z) + DT * (dil + 2.0 * mu * e)
        for f, e in ((6, exy), (7, exz), (8, eyz)):
            ext[f, pl.ds(16 * z, 16), :] = plane(ext, f, z) + DT * mu * e


def kernel(
    ngx,
    ngy,
    npart,
    state_in,
    lam_in,
    mu_in,
    buoy_in,
    scell_in,
    swave_in,
    start_in,
    weight_in,
    owner_in,
    chan_in,
    obs_in,
    res_out,
    grad_out,
    scell,
    swave,
    start,
    weight,
    owner,
    chan,
    obs,
    res,
    grad,
    own,
    xr,
    strip,
    yr,
    ext,
    mats,
    srcs,
    es,
    ad,
    glhs,
    colb,
    rank,
    win,
    lane1h,
    obs32,
    sa,
    ra,
    sx,
    rx,
    arr,
    chan1h,
    hirow,
    sx2,
    rx2,
    sa2,
    ra2,
    load,
    xr2,
    strip2,
    yr2,
    halo2,
    exl,
    hsend,
    hrecv,
    h2send,
    h2recv,
    esend,
    erecv,
    isem,
    osem,
    ready,
):
    gx, gy = lax.axis_index("gx"), lax.axis_index("gy")
    nchunk = npart // 128
    gy_bits = ngy.bit_length() - 1
    y_bits = gy_bits // 2
    ny = 1 << y_bits
    nx = ngy // ny
    right_x, left_x = lax.rem(gx + 1, ngx), lax.rem(gx + ngx - 1, ngx)
    right_y, left_y = lax.rem(gy + 1, ngy), lax.rem(gy + ngy - 1, ngy)
    first_x, last_x = gx == 0, gx == ngx - 1
    first_y, last_y = gy == 0, gy == ngy - 1

    if ngx < 16 or ngy < 64:
        for ref in (ra, rx, rx2, ra2):
            ref[...] = jnp.zeros_like(ref)

    barrier = pltpu.get_barrier_semaphore()

    def greet(x, y):
        pl.semaphore_signal(barrier, inc=1, device_id={"gx": x, "gy": y}, device_id_type=MESH)

    reads = [
        pltpu.make_async_copy(src, dst, isem.at[i])
        for i, (src, dst) in enumerate(
            (
                (state_in, own.at[pl.ds(0, 144)]),
                (scell_in, scell),
                (swave_in, swave),
                (buoy_in, own.at[pl.ds(144, 16)]),
                (lam_in, own.at[pl.ds(160, 16)]),
                (mu_in, own.at[pl.ds(176, 16)]),
                (owner_in, owner),
                (start_in, start),
                (chan_in, chan),
                (weight_in, weight),
                (obs_in, obs),
            )
        )
    ]
    for read in reads:
        read.start()

    def far_first(count):
        return sorted(range(1, count), key=lambda i: -min(i, count - i))

    def peer_z(i):
        return lax.rem(gx + i, ngx), gy

    def peer_x(i):
        return gx, lax.rem((gy >> y_bits) + i, nx) * ny + (gy & (ny - 1))

    def peer_y(i):
        return gx, (gy & ~(ny - 1)) + lax.rem((gy & (ny - 1)) + i, ny)

    greeted = [peer_z(i) for i in far_first(ngx)] + [peer_x(i) for i in far_first(nx)] + [peer_y(i) for i in far_first(ny)]
    greeted += [(x, y) for y in (left_y, right_y) for x in (gx, left_x, right_x)]
    for x, y in greeted:
        greet(x, y)

    mats[...] = jnp.zeros_like(mats)
    ext[...] = jnp.zeros_like(ext)
    exl[...] = jnp.zeros_like(exl)
    glhs[...] = jnp.zeros_like(glhs)
    obs32[...] = jnp.zeros_like(obs32)
    for read in reads[:6]:
        read.wait()

    cell = scell[...]
    nsrc = cell.shape[1]
    key = iota((48, nsrc), 0)
    wave = jnp.concatenate([jnp.broadcast_to(swave[t : t + 1, :], (16, nsrc)) for t in range(STEPS)], axis=0)
    lhs = jnp.where((key & 15) == (cell >> 7), wave, 0.0)
    srcs[...] = dot_split(lhs, ones_where(iota((128, nsrc), 0) == (cell & 127)), NT)
    for f in (3, 4, 5):
        own[16 * f : 16 * f + 16, :] = own[16 * f : 16 * f + 16, :] + srcs[0:16, :]
    own[192:224, :] = srcs[16:48, :]

    lane = iota((8, 128), 1)
    sub = iota((8, 128), 0)
    low4 = (lane & 7) < 4

    def pack(tile_of, groups, put):
        for u in range(-(-groups // 16)):
            acc = [jnp.zeros((8, 128), jnp.float32)] * 2
            for k in range(min(16, groups - 16 * u)):
                tile = tile_of(16 * u + k)
                here = (lane >> 3) == k
                acc[0] = jnp.where(here, pltpu.roll(tile, (8 * k - 124) % 128, 1), acc[0])
                acc[1] = jnp.where(here, pltpu.roll(tile, (8 * k + 4) % 128, 1), acc[1])
            for side in range(2):
                put(side, u, acc[side])

    def put_strip(side, u, value):
        strip[side, pl.ds(8 * u, 8), :] = value

    pack(lambda i: own[8 * i : 8 * i + 8, :], 2 * NF, put_strip)

    pl.semaphore_wait(barrier, len(greeted))
    for i in far_first(nx):
        x, y = peer_x(i)
        pl.semaphore_signal(ready, inc=1, device_id={"gx": x, "gy": y}, device_id_type=MESH)

    def halo_copies(rows, rows_to, strips, strips_to, send, recv):
        plan = [
            (rows, rows_to.at[0], right_x, gy),
            (rows, rows_to.at[1], left_x, gy),
            (strips.at[0], strips_to.at[1, 0], gx, right_y),
            (strips.at[1], strips_to.at[1, 1], gx, left_y),
            (strips.at[0], strips_to.at[0, 0], right_x, right_y),
            (strips.at[1], strips_to.at[0, 1], right_x, left_y),
            (strips.at[0], strips_to.at[2, 0], left_x, right_y),
            (strips.at[1], strips_to.at[2, 1], left_x, left_y),
        ]
        copies = [
            pltpu.make_async_remote_copy(
                src_ref=src,
                dst_ref=dst,
                send_sem=send.at[i],
                recv_sem=recv.at[i],
                device_id={"gx": x, "gy": y},
                device_id_type=MESH,
            )
            for i, (src, dst, x, y) in enumerate(plan)
        ]
        for copy in copies:
            copy.start()
        return copies

    copies = halo_copies(own, xr, strip, yr, hsend, hrecv)
    for read in reads[6:]:
        read.wait()

    ownf = owner[...].astype(jnp.float32)
    cols = jnp.concatenate([ownf, jnp.zeros((128 - nchunk, 128), jnp.float32)], axis=0).T
    for c in range(nchunk):
        colb[c] = jnp.broadcast_to(cols[:, c : c + 1], (128, 128))
    earlier = iota((128, 128), 0) < iota((128, 128), 1)

    @pl.loop(0, nchunk)
    def _(c):
        row = jnp.broadcast_to(owner[pl.ds(c, 1), :].astype(jnp.float32), (128, 128))
        same = jnp.where((colb[c] == row) & earlier, 1.0, 0.0)

        def more(q, count):
            hit = jnp.where(colb[q] == row, 1.0, 0.0)
            return count + hit.reshape(16, 8, 128).sum(axis=0)

        count = lax.fori_loop(0, c, more, same.reshape(16, 8, 128).sum(axis=0))
        rank[pl.ds(c, 1), :] = jnp.sum(count, axis=0, keepdims=True)

    for i in range(8):
        obs32[4 * i : 4 * i + 3, :] = obs[:, 128 * i : 128 * i + 128]


    def chunk_key(c, width):
        own_c = jnp.concatenate([owner[c + i : c + i + 1, :] for i in range(width)], axis=1)
        rank_c = jnp.concatenate([rank[c + i : c + i + 1, :] for i in range(width)], axis=1).astype(jnp.int32)
        return own_c, rank_c

    def row_of(c, width):
        start_c = jnp.concatenate([start[c + i : c + i + 1, :] for i in range(width)], axis=1)
        row_c = (start_c * 8666) >> 20
        return start_c, row_c

    for c in range(nchunk):
        start_c, row_c = row_of(c, 1)
        ahead_c = iota((128, 128), 0) - (start_c - 121 * row_c)
        win[:, 128 * c : 128 * c + 128] = ones_where((ahead_c >= 0) & (ahead_c < GAUGE))
        own_c, rank_c = chunk_key(c, 1)
        lane_c = (own_c & (ngy - 1)) * 2 + (rank_c & 1)
        lane1h[:, 128 * c : 128 * c + 128] = ones_where(iota((128, 128), 0) == lane_c)

    def place_rows(g, rows_ref, drop):
        for f in range(NF):
            for z in range(4):
                part = rows_ref[16 * f + 4 * z : 16 * f + 4 * z + 4, :]
                if drop is not None:
                    part = jnp.where(drop, 0.0, part)
                put_ext(f, slice(16 * z + 4 * g, 16 * z + 4 * g + 4), slice(0, 128), part)

    def put_ext(f, rows, lanes, value):
        if f < 9:
            ext[f, rows, lanes] = value
        elif f < 12:
            mats[f - 9, rows, lanes] = value
        else:
            exl[f - 12, rows, lanes] = value

    def comb(strips, g, u):
        low = jnp.where(first_y, 0.0, strips[g, 0, pl.ds(8 * u, 8), :])
        high = jnp.where(last_y, 0.0, strips[g, 1, pl.ds(8 * u, 8), :])
        both = jnp.where(low4, low, high)
        if g == 0:
            both = jnp.where(first_x, 0.0, both)
        if g == 2:
            both = jnp.where(last_x, 0.0, both)
        return both

    place_rows(1, own, None)
    for copy in copies:
        copy.wait()
    place_rows(0, xr.at[0], first_x)
    place_rows(2, xr.at[1], last_x)
    for g in range(3):
        for u in range(2):
            both = comb(yr, g, u)
            for k in range(min(16, 2 * NF - 16 * u)):
                f, h = divmod(16 * u + k, 2)
                tile = pltpu.roll(both, (124 - 8 * k) % 128, 1)
                for i in range(2):
                    z = 2 * h + i
                    put_ext(f, slice(16 * z + 4 * g, 16 * z + 4 * g + 4), slice(128, 256), tile[4 * i : 4 * i + 4, :])

    for t in range(STEPS):
        if t > 0:
            for f in (3, 4, 5):
                ext[f] = ext[f] + exl[t - 1]

        def emit(z, e, t=t):
            for i in range(6):
                es[6 * t + i, pl.ds(4 * z, 4), :] = e[i]
            for f in range(2):
                glhs[pl.ds(32 * z + 4 * f + t, 4, stride=8), :] = e[f]

        time_step(ext, mats, emit)

    def sub_of(width):
        return iota((8, width), 0)

    def weights(c, width):
        both = weight[:, 128 * c : 128 * (c + width)]
        return jnp.where(sub_of(128 * width) < 4, both[0:1, :], both[1:2, :])

    width = 2 if nchunk % 2 == 0 else 1
    wide = 128 * width
    by_four, by_eight = narrow(iota((128, wide), 0) >> 2), narrow(iota((128, wide), 0) >> 3)
    gpieces = jnp.concatenate(split(glhs[...]), axis=0)
    acc = jnp.zeros((PIECES * 128, 128), jnp.float32)
    for c in range(0, nchunk, width):
        lanes = slice(128 * c, 128 * c + wide)
        _, row_c = row_of(c, width)
        got = dot(gpieces, win[:, lanes], NN)
        picked = jnp.zeros((8, wide), jnp.float32)
        for r in range(16):
            tile = got[8 * r : 8 * r + 8]
            for i in range(1, PIECES):
                tile = tile + got[128 * i + 8 * r : 128 * i + 8 * r + 8]
            picked = picked + jnp.where(row_c == r, tile, 0.0)
        picked = picked * weights(c, width)
        picked = picked + pltpu.roll(picked, 4, 0)
        chan_c = jnp.concatenate([chan[c + i : c + i + 1, :] for i in range(width)], axis=1)
        picked = jnp.where((sub_of(wide) & 3) == 3, chan_c.astype(jnp.float32), picked)
        own_c, rank_c = chunk_key(c, width)
        key_c = (own_c >> gy_bits) * 2 + (rank_c >> 1)
        acc = acc + dot(spread_rows(picked, by_four, key_c, 8), lane1h[:, lanes], NT)
    total = acc[0:128]
    for i in range(1, PIECES):
        total = total + acc[128 * i : 128 * i + 128]
    sa[...] = total.reshape(16, 8, 128)

    def exchange(stage, peers, me, src, dst):
        send, recv = esend.at[stage], erecv.at[stage]
        for place, x, y in peers:
            pltpu.make_async_remote_copy(
                src_ref=src.at[place],
                dst_ref=dst.at[me],
                send_sem=send,
                recv_sem=recv,
                device_id={"gx": x, "gy": y},
                device_id_type=MESH,
            ).start()
        pltpu.make_async_copy(src.at[me], dst.at[me], recv).start()
        whole, less = dst.at[pl.ds(0, len(peers) + 1)], src.at[pl.ds(0, len(peers))]
        pltpu.make_async_copy(whole, whole, recv).wait()
        pltpu.make_async_copy(less, less, send).wait()

    z_peers = [(lax.rem(gx + i, ngx), lax.rem(gx + i, ngx), gy) for i in far_first(ngx)]
    xs = [lax.rem((gy >> y_bits) + i, nx) * ny for i in range(nx)]
    ys = [lax.rem((gy & (ny - 1)) + i, ny) for i in range(ny)]
    offsets = [(i, j) for i in range(nx) for j in range(ny) if i or j]
    offsets.sort(key=lambda o: -min(o[0], nx - o[0]) - min(o[1], ny - o[1]))
    xy_peers = [(xs[i] + ys[j], gx, xs[i] + ys[j]) for i, j in offsets]

    exchange(0, z_peers, gx, sa, ra)
    sx[...] = ra[...].reshape(128, 128).T.reshape(64, 2, 128)
    pl.semaphore_wait(ready, nx - 1)
    exchange(1, xy_peers, gy, sx, rx)
    arr[...] = rx[...].reshape(128, 128).T

    acc = jnp.zeros((PIECES * 32, 128), jnp.float32)
    sub256 = sub_of(256) >> 2
    rows256 = narrow(iota((128, 256), 0))
    one, none = jnp.ones((128, 256), jnp.bfloat16), jnp.zeros((128, 256), jnp.bfloat16)
    by_four32 = narrow(iota((32, 256), 0) >> 2)
    for d in range(16):
        tile = arr[8 * d : 8 * d + 8, :]
        turned = pltpu.roll(tile, 4, 0)
        both = jnp.concatenate([jnp.where(sub < 4, tile, turned), jnp.where(sub < 4, turned, tile)], axis=1)
        ids = both[3:4, :].astype(jnp.int32)
        onehot = jnp.where(rows256 == narrow(ids & 127), one, none)
        chan1h[:, 256 * d : 256 * d + 256] = onehot
        hi = ids >> 7
        hirow[d : d + 1, :] = hi
        acc = acc + dot(spread_rows(both, by_four32, hi, 2), onehot, NT)
    sums = acc[0:32]
    for i in range(1, PIECES):
        sums = sums + acc[32 * i : 32 * i + 32]
    sums = jnp.where((iota((32, 128), 0) & 3) == 3, 0.0, sums - obs32[...])
    for i in range(8):
        res[:, 128 * i : 128 * i + 128] = sums[4 * i : 4 * i + 3, :]
    put_res = pltpu.make_async_copy(res, res_out, osem.at[0])
    put_res.start()

    pieces = jnp.concatenate(split(sums), axis=0)
    for d in range(16):
        got = dot(pieces, chan1h[:, 256 * d : 256 * d + 256], NN)
        hi = hirow[d : d + 1, :]
        picked = jnp.zeros((8, 256), jnp.float32)
        for j in range(4):
            tile = got[8 * j : 8 * j + 8]
            for i in range(1, PIECES):
                tile = tile + got[32 * i + 8 * j : 32 * i + 8 * j + 8]
            picked = picked + jnp.where(hi == sub256 + 2 * j, tile, 0.0)
        picked = picked + pltpu.roll(picked, 4, 0)
        arr[8 * d : 8 * d + 8, :] = jnp.where(sub < 4, picked[:, 0:128], picked[:, 128:256])
    sx2[...] = arr[...].T.reshape(64, 2, 128)
    exchange(2, xy_peers, gy, sx2, rx2)
    sa2[...] = rx2[...].reshape(128, 128).T.reshape(16, 8, 128)
    exchange(3, z_peers, gx, sa2, ra2)

    pieces = jnp.concatenate(split(ra2[...].reshape(128, 128)), axis=0)
    acc = jnp.zeros((PIECES * 128, 128), jnp.float32)
    for c in range(0, nchunk, width):
        lanes = slice(128 * c, 128 * c + wide)
        got = dot(pieces, lane1h[:, lanes], NN)
        own_c, rank_c = chunk_key(c, width)
        key_c = (own_c >> gy_bits) * 2 + (rank_c >> 1)
        half = sub_of(wide) >> 2
        picked = jnp.zeros((8, wide), jnp.float32)
        for r in range(16):
            tile = got[8 * r : 8 * r + 8]
            for i in range(1, PIECES):
                tile = tile + got[128 * i + 8 * r : 128 * i + 8 * r + 8]
            picked = picked + jnp.where(key_c == half + 2 * r, tile, 0.0)
        picked = (picked + pltpu.roll(picked, 4, 0)) * weights(c, width)
        _, row_c = row_of(c, width)
        acc = acc + dot(spread_rows(picked, by_eight, row_c, 8), win[:, lanes], NT)
    total = acc[0:128]
    for i in range(1, PIECES):
        total = total + acc[128 * i : 128 * i + 128]
    load[...] = total

    def put_strip2(side, u, value):
        strip2[side] = value

    pack(lambda i: load[8 * i : 8 * i + 8, :], 16, put_strip2)
    copies = halo_copies(load, xr2, strip2, yr2, h2send, h2recv)
    ext[...] = jnp.zeros_like(ext)
    for copy in copies:
        copy.wait()
    for g in range(3):
        both = comb(yr2, g, 0)
        for k in range(16):
            halo2[g, pl.ds(8 * k, 8), :] = pltpu.roll(both, (124 - 8 * k) % 128, 1)
    sources = ((xr2.at[0], first_x), (load, None), (xr2.at[1], last_x))
    for f in range(2):
        for t in range(STEPS):
            for z in range(4):
                rows = pl.ds(32 * z + 4 * f + t, 4, stride=8)
                for g, (ref, drop) in enumerate(sources):
                    part = ref[rows, :]
                    if drop is not None:
                        part = jnp.where(drop, 0.0, part)
                    exl[2 * t + f, 16 * z + 4 * g : 16 * z + 4 * g + 4, 0:128] = part
                    exl[2 * t + f, 16 * z + 4 * g : 16 * z + 4 * g + 4, 128:256] = halo2[g, rows, :]

    lam_grad = jnp.zeros((16, 128), jnp.float32)
    mu_grad = jnp.zeros((16, 128), jnp.float32)
    for k in range(STEPS):
        t = STEPS - 1 - k
        for f in range(2):
            ext[3 + f] = ext[3 + f] + exl[2 * t + f]

        def emit(z, e):
            for i in range(6):
                ad[i, pl.ds(4 * z, 4), :] = e[i]

        time_step(ext, mats, emit)
        fwd = [es[6 * t + i] for i in range(6)]
        adj = [ad[i] for i in range(6)]
        prod = [a * b for a, b in zip(fwd, adj)]
        lam_grad = lam_grad + (fwd[0] + fwd[1] + fwd[2]) * (adj[0] + adj[1] + adj[2])
        mu_grad = mu_grad + (2.0 * (prod[0] + prod[1] + prod[2]) + prod[3] + prod[4] + prod[5])
    grad[0:16, :] = lam_grad
    grad[16:32, :] = mu_grad
    put_grad = pltpu.make_async_copy(grad, grad_out, osem.at[1])
    put_grad.start()
    put_res.wait()
    put_grad.wait()


def publish(res_in, grad_in, res_out, grad_out, sem):
    copies = [
        pltpu.make_async_copy(res_in, res_out, sem.at[0]),
        pltpu.make_async_copy(grad_in, grad_out, sem.at[1]),
    ]
    for copy in copies:
        copy.start()
    for copy in copies:
        copy.wait()


def shards(
    initial_state,
    lame_lambda,
    shear_modulus,
    buoyancy,
    source_cells,
    source_wavelet,
    segment_start,
    segment_weight,
    partial_owner,
    partial_channel,
    observed_data,
):
    ngx, ngy = lax.axis_size("gx"), lax.axis_size("gy")
    npart = segment_start.shape[0]
    nsrc = source_cells.shape[0]
    f32, bf16 = jnp.float32, jnp.bfloat16
    anywhere = pl.BlockSpec(memory_space=pl.ANY)
    dma = pltpu.SemaphoreType.DMA
    scratch = [
        pltpu.VMEM((1, nsrc), jnp.int32),
        pltpu.VMEM((STEPS, nsrc), f32),
        pltpu.VMEM((npart // 128, 128), jnp.int32),
        pltpu.VMEM((2, npart), f32),
        pltpu.VMEM((npart // 128, 128), jnp.int32),
        pltpu.VMEM((npart // 128, 128), jnp.int32),
        pltpu.VMEM(observed_data.shape, f32),
        pltpu.VMEM(observed_data.shape, f32),
        pltpu.VMEM((32, 128), f32),
        pltpu.VMEM((16 * NF, 128), f32),
        pltpu.VMEM((2, 16 * NF, 128), f32),
        pltpu.VMEM((2, 16, 128), f32),
        pltpu.VMEM((3, 2, 16, 128), f32),
        pltpu.VMEM((9, 64, 256), f32),
        pltpu.VMEM((3, 64, 256), f32),
        pltpu.VMEM((48, 128), f32),
        pltpu.VMEM((6 * STEPS, 16, 128), f32),
        pltpu.VMEM((6, 16, 128), f32),
        pltpu.VMEM((128, 128), f32),
        pltpu.VMEM((npart // 128, 128, 128), f32),
        pltpu.VMEM((npart // 128, 128), f32),
        pltpu.VMEM((128, npart), bf16),
        pltpu.VMEM((128, npart), bf16),
        pltpu.VMEM((32, 128), f32),
        pltpu.VMEM((16, 8, 128), f32),
        pltpu.VMEM((16, 8, 128), f32),
        pltpu.VMEM((64, 2, 128), f32),
        pltpu.VMEM((64, 2, 128), f32),
        pltpu.VMEM((128, 128), f32),
        pltpu.VMEM((128, 4096), bf16),
        pltpu.VMEM((16, 256), jnp.int32),
        pltpu.VMEM((64, 2, 128), f32),
        pltpu.VMEM((64, 2, 128), f32),
        pltpu.VMEM((16, 8, 128), f32),
        pltpu.VMEM((16, 8, 128), f32),
        pltpu.VMEM((128, 128), f32),
        pltpu.VMEM((2, 128, 128), f32),
        pltpu.VMEM((2, 8, 128), f32),
        pltpu.VMEM((3, 2, 8, 128), f32),
        pltpu.VMEM((3, 128, 128), f32),
        pltpu.VMEM((2 * STEPS, 64, 256), f32),
        dma((8,)),
        dma((8,)),
        dma((8,)),
        dma((8,)),
        dma((4,)),
        dma((4,)),
        dma((11,)),
        dma((2,)),
        pltpu.SemaphoreType.REGULAR,
    ]
    residuals, gradients = pl.pallas_call(
        functools.partial(kernel, ngx, ngy, npart),
        out_shape=(
            jax.ShapeDtypeStruct(observed_data.shape, f32),
            jax.ShapeDtypeStruct((32, 128), f32),
        ),
        in_specs=[anywhere] * 11,
        out_specs=(anywhere, anywhere),
        scratch_shapes=scratch,
        compiler_params=pltpu.CompilerParams(collective_id=0, has_side_effects=True, vmem_limit_bytes=25165824),
        name="window",
    )(
        *[pltpu.with_memory_space_constraint(x, pltpu.HBM) for x in (
        initial_state.reshape(144, 128),
        lame_lambda.reshape(16, 128),
        shear_modulus.reshape(16, 128),
        buoyancy.reshape(16, 128),
        source_cells.reshape(1, nsrc),
        source_wavelet,
        segment_start.reshape(-1, 128),
        segment_weight,
        partial_owner.reshape(-1, 128),
        partial_channel.reshape(-1, 128),
        observed_data)],
    )
    residuals, gradients = pl.pallas_call(
        publish,
        out_shape=(jax.ShapeDtypeStruct(observed_data.shape, f32), jax.ShapeDtypeStruct((32, 128), f32)),
        in_specs=[anywhere, anywhere],
        out_specs=(anywhere, anywhere),
        scratch_shapes=[dma((2,))],
        compiler_params=pltpu.CompilerParams(vmem_limit_bytes=1 << 20),
        name="publish",
    )(residuals, gradients)
    return residuals, gradients.reshape(2, 4, 4, 128)


def solution(mesh):
    in_specs = (
        P(None, None, "gx", "gy"),
        P(None, "gx", "gy"),
        P(None, "gx", "gy"),
        P(None, "gx", "gy"),
        P(("gx", "gy")),
        P(None, ("gx", "gy")),
        P(("gx", "gy")),
        P(None, ("gx", "gy")),
        P(("gx", "gy"), None),
        P(("gx", "gy")),
        P(None, ("gx", "gy")),
    )
    out_specs = (P(None, ("gx", "gy")), P(None, None, "gx", "gy"))
    return jax.shard_map(shards, mesh=mesh, in_specs=in_specs, out_specs=out_specs, check_vma=False)
```

```python
import functools

import jax
import jax.numpy as jnp
from jax import lax
from jax.experimental import pallas as pl
from jax.experimental.pallas import tpu as pltpu
from jax.sharding import PartitionSpec as P

GAUGE = 8
DT = 0.25
PIECES = 3
STEPS = 3
NF = 14
MESH = pl.DeviceIdType.MESH
NT = (((1,), (1,)), ((), ()))
NN = (((1,), (0,)), ((), ()))


def iota(shape, dim):
    return lax.broadcasted_iota(jnp.int32, shape, dim)


def split(x):
    parts = []
    for _ in range(PIECES):
        part = x.astype(jnp.bfloat16)
        parts.append(part)
        x = x - part.astype(jnp.float32)
    return parts


def dot(a, b, dims):
    return lax.dot_general(a, b, dims, preferred_element_type=jnp.float32)


def dot_split(x, b, dims):
    parts = split(x)
    rows = x.shape[0]
    stacked = dot(jnp.concatenate(parts, axis=0), b, dims)
    total = stacked[:rows]
    for i in range(1, PIECES):
        total = total + stacked[i * rows : (i + 1) * rows]
    return total


def ones_where(mask):
    return jnp.where(mask, 1.0, 0.0).astype(jnp.bfloat16)


def narrow(x):
    return x.astype(jnp.float32).astype(jnp.bfloat16)


def spread_rows(x, key_rows, key, copies):
    hit = key_rows == narrow(key)
    zero = jnp.zeros(hit.shape, jnp.bfloat16)
    pieces = split(jnp.concatenate([x, x], axis=0))
    return jnp.concatenate(
        [jnp.where(hit, jnp.concatenate([piece] * copies, axis=0), zero) for piece in pieces], axis=0
    )


def ahead(f, axis):
    return pltpu.roll(f, f.shape[axis] - 1, axis) - f


def behind(f, axis):
    return f - pltpu.roll(f, 1, axis)


def time_step(ext, mats, emit):
    def plane(ref, f, z):
        return ref[f, pl.ds(16 * z, 16), :]

    def ahead_z(f, z):
        return (plane(ext, f, z + 1) if z < 3 else 0.0) - plane(ext, f, z)

    def behind_z(f, z):
        here = plane(ext, f, z)
        return here - plane(ext, f, z - 1) if z > 0 else here

    for z in range(4):
        scale = DT * plane(mats, 0, z)
        sxy, sxz, syz = plane(ext, 6, z), plane(ext, 7, z), plane(ext, 8, z)
        ax = ahead(plane(ext, 3, z), 0) + behind(sxy, 1) + behind_z(7, z)
        ay = behind(sxy, 0) + ahead(plane(ext, 4, z), 1) + behind_z(8, z)
        az = behind(sxz, 0) + behind(syz, 1) + ahead_z(5, z)
        for f, a in enumerate((ax, ay, az)):
            ext[f, pl.ds(16 * z, 16), :] = plane(ext, f, z) + scale * a
    for z in range(4):
        vx, vy, vz = plane(ext, 0, z), plane(ext, 1, z), plane(ext, 2, z)
        exx = behind(vx, 0)
        eyy = behind(vy, 1)
        ezz = behind_z(2, z)
        exy = ahead(vx, 1) + ahead(vy, 0)
        exz = ahead_z(0, z) + ahead(vz, 0)
        eyz = ahead_z(1, z) + ahead(vz, 1)
        emit(z, [e[4:8, 0:128] for e in (exx, eyy, ezz, exy, exz, eyz)])
        lam, mu = plane(mats, 1, z), plane(mats, 2, z)
        dil = lam * (exx + eyy + ezz)
        for f, e in ((3, exx), (4, eyy), (5, ezz)):
            ext[f, pl.ds(16 * z, 16), :] = plane(ext, f, z) + DT * (dil + 2.0 * mu * e)
        for f, e in ((6, exy), (7, exz), (8, eyz)):
            ext[f, pl.ds(16 * z, 16), :] = plane(ext, f, z) + DT * mu * e


def kernel(
    ngx,
    ngy,
    npart,
    state_in,
    lam_in,
    mu_in,
    buoy_in,
    scell_in,
    swave_in,
    start_in,
    weight_in,
    owner_in,
    chan_in,
    obs_in,
    res_out,
    grad_out,
    scell,
    swave,
    start,
    weight,
    owner,
    chan,
    obs,
    own,
    xr,
    strip,
    yr,
    ext,
    mats,
    srcs,
    es,
    ad,
    glhs,
    colb,
    rank,
    win,
    lane1h,
    obs32,
    sa,
    ra,
    sx,
    rx,
    arr,
    chan1h,
    hirow,
    sx2,
    rx2,
    sa2,
    ra2,
    load,
    xr2,
    strip2,
    yr2,
    halo2,
    exl,
    hsend,
    hrecv,
    h2send,
    h2recv,
    esend,
    erecv,
    isem,
    ready,
):
    gx, gy = lax.axis_index("gx"), lax.axis_index("gy")
    nchunk = npart // 128
    gy_bits = ngy.bit_length() - 1
    y_bits = gy_bits // 2
    ny = 1 << y_bits
    nx = ngy // ny
    right_x, left_x = lax.rem(gx + 1, ngx), lax.rem(gx + ngx - 1, ngx)
    right_y, left_y = lax.rem(gy + 1, ngy), lax.rem(gy + ngy - 1, ngy)
    first_x, last_x = gx == 0, gx == ngx - 1
    first_y, last_y = gy == 0, gy == ngy - 1

    if ngx < 16 or ngy < 64:
        for ref in (ra, rx, rx2, ra2):
            ref[...] = jnp.zeros_like(ref)

    barrier = pltpu.get_barrier_semaphore()

    def greet(x, y):
        pl.semaphore_signal(barrier, inc=1, device_id={"gx": x, "gy": y}, device_id_type=MESH)

    reads = [
        pltpu.make_async_copy(src, dst, isem.at[i])
        for i, (src, dst) in enumerate(
            (
                (state_in, own.at[pl.ds(0, 144)]),
                (scell_in, scell),
                (swave_in, swave),
                (buoy_in, own.at[pl.ds(144, 16)]),
                (lam_in, own.at[pl.ds(160, 16)]),
                (mu_in, own.at[pl.ds(176, 16)]),
                (owner_in, owner),
                (start_in, start),
                (chan_in, chan),
                (weight_in, weight),
                (obs_in, obs),
            )
        )
    ]
    for read in reads:
        read.start()

    def far_first(count):
        return sorted(range(1, count), key=lambda i: -min(i, count - i))

    def peer_z(i):
        return lax.rem(gx + i, ngx), gy

    def peer_x(i):
        return gx, lax.rem((gy >> y_bits) + i, nx) * ny + (gy & (ny - 1))

    def peer_y(i):
        return gx, (gy & ~(ny - 1)) + lax.rem((gy & (ny - 1)) + i, ny)

    greeted = [peer_z(i) for i in far_first(ngx)] + [peer_x(i) for i in far_first(nx)] + [peer_y(i) for i in far_first(ny)]
    greeted += [(x, y) for y in (left_y, right_y) for x in (gx, left_x, right_x)]
    for x, y in greeted:
        greet(x, y)

    mats[...] = jnp.zeros_like(mats)
    ext[...] = jnp.zeros_like(ext)
    exl[...] = jnp.zeros_like(exl)
    glhs[...] = jnp.zeros_like(glhs)
    obs32[...] = jnp.zeros_like(obs32)
    for read in reads[:7]:
        read.wait()

    cell = scell[...]
    nsrc = cell.shape[1]
    key = iota((48, nsrc), 0)
    wave = jnp.concatenate([jnp.broadcast_to(swave[t : t + 1, :], (16, nsrc)) for t in range(STEPS)], axis=0)
    lhs = jnp.where((key & 15) == (cell >> 7), wave, 0.0)
    srcs[...] = dot_split(lhs, ones_where(iota((128, nsrc), 0) == (cell & 127)), NT)
    for f in (3, 4, 5):
        own[16 * f : 16 * f + 16, :] = own[16 * f : 16 * f + 16, :] + srcs[0:16, :]
    own[192:224, :] = srcs[16:48, :]

    lane = iota((8, 128), 1)
    sub = iota((8, 128), 0)
    low4 = (lane & 7) < 4

    def pack(tile_of, groups, put):
        for u in range(-(-groups // 16)):
            acc = [jnp.zeros((8, 128), jnp.float32)] * 2
            for k in range(min(16, groups - 16 * u)):
                tile = tile_of(16 * u + k)
                here = (lane >> 3) == k
                acc[0] = jnp.where(here, pltpu.roll(tile, (8 * k - 124) % 128, 1), acc[0])
                acc[1] = jnp.where(here, pltpu.roll(tile, (8 * k + 4) % 128, 1), acc[1])
            for side in range(2):
                put(side, u, acc[side])

    def put_strip(side, u, value):
        strip[side, pl.ds(8 * u, 8), :] = value

    pack(lambda i: own[8 * i : 8 * i + 8, :], 2 * NF, put_strip)

    ownf = owner[...].astype(jnp.float32)
    cols = jnp.concatenate([ownf, jnp.zeros((128 - nchunk, 128), jnp.float32)], axis=0).T
    for c in range(nchunk):
        colb[c] = jnp.broadcast_to(cols[:, c : c + 1], (128, 128))
    earlier = iota((128, 128), 0) < iota((128, 128), 1)

    def rank_chunk(c):
        row = jnp.broadcast_to(owner[pl.ds(c, 1), :].astype(jnp.float32), (128, 128))
        same = jnp.where((colb[c] == row) & earlier, 1.0, 0.0)

        def more(q, count):
            hit = jnp.where(colb[q] == row, 1.0, 0.0)
            return count + hit.reshape(16, 8, 128).sum(axis=0)

        count = lax.fori_loop(0, c, more, same.reshape(16, 8, 128).sum(axis=0))
        rank[pl.ds(c, 1), :] = jnp.sum(count, axis=0, keepdims=True)

    halfway = nchunk * 11 // 16
    pl.loop(0, halfway)(rank_chunk)

    pl.semaphore_wait(barrier, len(greeted))
    for i in far_first(nx):
        x, y = peer_x(i)
        pl.semaphore_signal(ready, inc=1, device_id={"gx": x, "gy": y}, device_id_type=MESH)

    def halo_copies(rows, rows_to, strips, strips_to, send, recv):
        plan = [
            (strips.at[0], strips_to.at[0, 0], right_x, right_y),
            (strips.at[1], strips_to.at[0, 1], right_x, left_y),
            (strips.at[0], strips_to.at[2, 0], left_x, right_y),
            (strips.at[1], strips_to.at[2, 1], left_x, left_y),
            (strips.at[0], strips_to.at[1, 0], gx, right_y),
            (strips.at[1], strips_to.at[1, 1], gx, left_y),
            (rows, rows_to.at[0], right_x, gy),
            (rows, rows_to.at[1], left_x, gy),
        ]
        copies = [
            pltpu.make_async_remote_copy(
                src_ref=src,
                dst_ref=dst,
                send_sem=send.at[i],
                recv_sem=recv.at[i],
                device_id={"gx": x, "gy": y},
                device_id_type=MESH,
            )
            for i, (src, dst, x, y) in enumerate(plan)
        ]
        for copy in copies:
            copy.start()
        return copies

    copies = halo_copies(own, xr, strip, yr, hsend, hrecv)
    for read in reads[7:]:
        read.wait()

    pl.loop(halfway, nchunk)(rank_chunk)

    for i in range(8):
        obs32[4 * i : 4 * i + 3, :] = obs[:, 128 * i : 128 * i + 128]


    def chunk_key(c, width):
        own_c = jnp.concatenate([owner[c + i : c + i + 1, :] for i in range(width)], axis=1)
        rank_c = jnp.concatenate([rank[c + i : c + i + 1, :] for i in range(width)], axis=1).astype(jnp.int32)
        return own_c, rank_c

    def row_of(c, width):
        start_c = jnp.concatenate([start[c + i : c + i + 1, :] for i in range(width)], axis=1)
        row_c = (start_c * 8666) >> 20
        return start_c, row_c

    for c in range(nchunk):
        start_c, row_c = row_of(c, 1)
        ahead_c = iota((128, 128), 0) - (start_c - 121 * row_c)
        win[:, 128 * c : 128 * c + 128] = ones_where((ahead_c >= 0) & (ahead_c < GAUGE))
        own_c, rank_c = chunk_key(c, 1)
        lane_c = (own_c & (ngy - 1)) * 2 + (rank_c & 1)
        lane1h[:, 128 * c : 128 * c + 128] = ones_where(iota((128, 128), 0) == lane_c)

    def place_rows(g, rows_ref, drop):
        for f in range(NF):
            for z in range(4):
                part = rows_ref[16 * f + 4 * z : 16 * f + 4 * z + 4, :]
                if drop is not None:
                    part = jnp.where(drop, 0.0, part)
                put_ext(f, slice(16 * z + 4 * g, 16 * z + 4 * g + 4), slice(0, 128), part)

    def put_ext(f, rows, lanes, value):
        if f < 9:
            ext[f, rows, lanes] = value
        elif f < 12:
            mats[f - 9, rows, lanes] = value
        else:
            exl[f - 12, rows, lanes] = value

    def comb(strips, g, u):
        low = jnp.where(first_y, 0.0, strips[g, 0, pl.ds(8 * u, 8), :])
        high = jnp.where(last_y, 0.0, strips[g, 1, pl.ds(8 * u, 8), :])
        both = jnp.where(low4, low, high)
        if g == 0:
            both = jnp.where(first_x, 0.0, both)
        if g == 2:
            both = jnp.where(last_x, 0.0, both)
        return both

    place_rows(1, own, None)
    for copy in copies:
        copy.wait()
    place_rows(0, xr.at[0], first_x)
    place_rows(2, xr.at[1], last_x)
    for g in range(3):
        for u in range(2):
            both = comb(yr, g, u)
            for k in range(min(16, 2 * NF - 16 * u)):
                f, h = divmod(16 * u + k, 2)
                tile = pltpu.roll(both, (124 - 8 * k) % 128, 1)
                for i in range(2):
                    z = 2 * h + i
                    put_ext(f, slice(16 * z + 4 * g, 16 * z + 4 * g + 4), slice(128, 256), tile[4 * i : 4 * i + 4, :])

    for t in range(STEPS):
        if t > 0:
            for f in (3, 4, 5):
                ext[f] = ext[f] + exl[t - 1]

        def emit(z, e, t=t):
            for i in range(6):
                es[6 * t + i, pl.ds(4 * z, 4), :] = e[i]
            for f in range(2):
                glhs[pl.ds(32 * z + 4 * f + t, 4, stride=8), :] = e[f]

        time_step(ext, mats, emit)

    def sub_of(width):
        return iota((8, width), 0)

    def weights(c, width):
        both = weight[:, 128 * c : 128 * (c + width)]
        return jnp.where(sub_of(128 * width) < 4, both[0:1, :], both[1:2, :])

    width = 2 if nchunk % 2 == 0 else 1
    wide = 128 * width
    by_four, by_eight = narrow(iota((128, wide), 0) >> 2), narrow(iota((128, wide), 0) >> 3)
    gpieces = jnp.concatenate(split(glhs[...]), axis=0)
    acc = jnp.zeros((PIECES * 128, 128), jnp.float32)
    for c in range(0, nchunk, width):
        lanes = slice(128 * c, 128 * c + wide)
        _, row_c = row_of(c, width)
        got = dot(gpieces, win[:, lanes], NN)
        picked = jnp.zeros((8, wide), jnp.float32)
        for r in range(16):
            tile = got[8 * r : 8 * r + 8]
            for i in range(1, PIECES):
                tile = tile + got[128 * i + 8 * r : 128 * i + 8 * r + 8]
            picked = picked + jnp.where(row_c == r, tile, 0.0)
        picked = picked * weights(c, width)
        picked = picked + pltpu.roll(picked, 4, 0)
        chan_c = jnp.concatenate([chan[c + i : c + i + 1, :] for i in range(width)], axis=1)
        picked = jnp.where((sub_of(wide) & 3) == 3, chan_c.astype(jnp.float32), picked)
        own_c, rank_c = chunk_key(c, width)
        key_c = (own_c >> gy_bits) * 2 + (rank_c >> 1)
        acc = acc + dot(spread_rows(picked, by_four, key_c, 8), lane1h[:, lanes], NT)
    total = acc[0:128]
    for i in range(1, PIECES):
        total = total + acc[128 * i : 128 * i + 128]
    sa[...] = total.reshape(16, 8, 128)

    def exchange(stage, peers, me, src, dst):
        send, recv = esend.at[stage], erecv.at[stage]
        for place, x, y in peers:
            pltpu.make_async_remote_copy(
                src_ref=src.at[place],
                dst_ref=dst.at[me],
                send_sem=send,
                recv_sem=recv,
                device_id={"gx": x, "gy": y},
                device_id_type=MESH,
            ).start()
        pltpu.make_async_copy(src.at[me], dst.at[me], recv).start()
        whole, less = dst.at[pl.ds(0, len(peers) + 1)], src.at[pl.ds(0, len(peers))]
        pltpu.make_async_copy(whole, whole, recv).wait()
        pltpu.make_async_copy(less, less, send).wait()

    z_peers = [(lax.rem(gx + i, ngx), lax.rem(gx + i, ngx), gy) for i in far_first(ngx)]
    xs = [lax.rem((gy >> y_bits) + i, nx) * ny for i in range(nx)]
    ys = [lax.rem((gy & (ny - 1)) + i, ny) for i in range(ny)]
    offsets = [(i, j) for i in range(nx) for j in range(ny) if i or j]
    offsets.sort(key=lambda o: -min(o[0], nx - o[0]) - min(o[1], ny - o[1]))
    xy_peers = [(xs[i] + ys[j], gx, xs[i] + ys[j]) for i, j in offsets]

    exchange(0, z_peers, gx, sa, ra)
    sx[...] = ra[...].reshape(128, 128).T.reshape(64, 2, 128)
    pl.semaphore_wait(ready, nx - 1)
    exchange(1, xy_peers, gy, sx, rx)
    arr[...] = rx[...].reshape(128, 128).T

    acc = jnp.zeros((PIECES * 32, 128), jnp.float32)
    sub256 = sub_of(256) >> 2
    rows256 = narrow(iota((128, 256), 0))
    one, none = jnp.ones((128, 256), jnp.bfloat16), jnp.zeros((128, 256), jnp.bfloat16)
    by_four32 = narrow(iota((32, 256), 0) >> 2)
    for d in range(16):
        tile = arr[8 * d : 8 * d + 8, :]
        turned = pltpu.roll(tile, 4, 0)
        both = jnp.concatenate([jnp.where(sub < 4, tile, turned), jnp.where(sub < 4, turned, tile)], axis=1)
        ids = both[3:4, :].astype(jnp.int32)
        onehot = jnp.where(rows256 == narrow(ids & 127), one, none)
        chan1h[:, 256 * d : 256 * d + 256] = onehot
        hi = ids >> 7
        hirow[d : d + 1, :] = hi
        acc = acc + dot(spread_rows(both, by_four32, hi, 2), onehot, NT)
    sums = acc[0:32]
    for i in range(1, PIECES):
        sums = sums + acc[32 * i : 32 * i + 32]
    sums = jnp.where((iota((32, 128), 0) & 3) == 3, 0.0, sums - obs32[...])
    for i in range(8):
        res_out[:, 128 * i : 128 * i + 128] = sums[4 * i : 4 * i + 3, :]

    pieces = jnp.concatenate(split(sums), axis=0)
    for d in range(16):
        got = dot(pieces, chan1h[:, 256 * d : 256 * d + 256], NN)
        hi = hirow[d : d + 1, :]
        picked = jnp.zeros((8, 256), jnp.float32)
        for j in range(4):
            tile = got[8 * j : 8 * j + 8]
            for i in range(1, PIECES):
                tile = tile + got[32 * i + 8 * j : 32 * i + 8 * j + 8]
            picked = picked + jnp.where(hi == sub256 + 2 * j, tile, 0.0)
        picked = picked + pltpu.roll(picked, 4, 0)
        arr[8 * d : 8 * d + 8, :] = jnp.where(sub < 4, picked[:, 0:128], picked[:, 128:256])
    sx2[...] = arr[...].T.reshape(64, 2, 128)
    exchange(2, xy_peers, gy, sx2, rx2)
    sa2[...] = rx2[...].reshape(128, 128).T.reshape(16, 8, 128)
    exchange(3, z_peers, gx, sa2, ra2)

    pieces = jnp.concatenate(split(ra2[...].reshape(128, 128)), axis=0)
    acc = jnp.zeros((PIECES * 128, 128), jnp.float32)
    for c in range(0, nchunk, width):
        lanes = slice(128 * c, 128 * c + wide)
        got = dot(pieces, lane1h[:, lanes], NN)
        own_c, rank_c = chunk_key(c, width)
        key_c = (own_c >> gy_bits) * 2 + (rank_c >> 1)
        half = sub_of(wide) >> 2
        picked = jnp.zeros((8, wide), jnp.float32)
        for r in range(16):
            tile = got[8 * r : 8 * r + 8]
            for i in range(1, PIECES):
                tile = tile + got[128 * i + 8 * r : 128 * i + 8 * r + 8]
            picked = picked + jnp.where(key_c == half + 2 * r, tile, 0.0)
        picked = (picked + pltpu.roll(picked, 4, 0)) * weights(c, width)
        _, row_c = row_of(c, width)
        acc = acc + dot(spread_rows(picked, by_eight, row_c, 8), win[:, lanes], NT)
    total = acc[0:128]
    for i in range(1, PIECES):
        total = total + acc[128 * i : 128 * i + 128]
    load[...] = total

    def put_strip2(side, u, value):
        strip2[side] = value

    pack(lambda i: load[8 * i : 8 * i + 8, :], 16, put_strip2)
    copies = halo_copies(load, xr2, strip2, yr2, h2send, h2recv)
    ext[...] = jnp.zeros_like(ext)

    def place_loads(g, ref, drop):
        for f in range(2):
            for t in range(STEPS):
                for z in range(4):
                    part = ref[pl.ds(32 * z + 4 * f + t, 4, stride=8), :]
                    if drop is not None:
                        part = jnp.where(drop, 0.0, part)
                    exl[2 * t + f, 16 * z + 4 * g : 16 * z + 4 * g + 4, 0:128] = part

    place_loads(1, load, None)
    for copy in copies:
        copy.wait()
    place_loads(0, xr2.at[0], first_x)
    place_loads(2, xr2.at[1], last_x)
    for g in range(3):
        both = comb(yr2, g, 0)
        for k in range(16):
            halo2[g, pl.ds(8 * k, 8), :] = pltpu.roll(both, (124 - 8 * k) % 128, 1)
    for f in range(2):
        for t in range(STEPS):
            for z in range(4):
                rows = pl.ds(32 * z + 4 * f + t, 4, stride=8)
                for g in range(3):
                    exl[2 * t + f, 16 * z + 4 * g : 16 * z + 4 * g + 4, 128:256] = halo2[g, rows, :]

    lam_grad = jnp.zeros((16, 128), jnp.float32)
    mu_grad = jnp.zeros((16, 128), jnp.float32)
    for k in range(STEPS):
        t = STEPS - 1 - k
        for f in range(2):
            ext[3 + f] = ext[3 + f] + exl[2 * t + f]

        def emit(z, e):
            for i in range(6):
                ad[i, pl.ds(4 * z, 4), :] = e[i]

        time_step(ext, mats, emit)
        fwd = [es[6 * t + i] for i in range(6)]
        adj = [ad[i] for i in range(6)]
        prod = [a * b for a, b in zip(fwd, adj)]
        lam_grad = lam_grad + (fwd[0] + fwd[1] + fwd[2]) * (adj[0] + adj[1] + adj[2])
        mu_grad = mu_grad + (2.0 * (prod[0] + prod[1] + prod[2]) + prod[3] + prod[4] + prod[5])
    grad_out[0:16, :] = lam_grad
    grad_out[16:32, :] = mu_grad


def publish(res_in, grad_in, res_out, grad_out, sem):
    copies = [
        pltpu.make_async_copy(res_in, res_out, sem.at[0]),
        pltpu.make_async_copy(grad_in, grad_out, sem.at[1]),
    ]
    for copy in copies:
        copy.start()
    for copy in copies:
        copy.wait()


def shards(
    initial_state,
    lame_lambda,
    shear_modulus,
    buoyancy,
    source_cells,
    source_wavelet,
    segment_start,
    segment_weight,
    partial_owner,
    partial_channel,
    observed_data,
):
    ngx, ngy = lax.axis_size("gx"), lax.axis_size("gy")
    npart = segment_start.shape[0]
    nsrc = source_cells.shape[0]
    f32, bf16 = jnp.float32, jnp.bfloat16
    anywhere = pl.BlockSpec(memory_space=pl.ANY)
    dma = pltpu.SemaphoreType.DMA
    scratch = [
        pltpu.VMEM((1, nsrc), jnp.int32),
        pltpu.VMEM((STEPS, nsrc), f32),
        pltpu.VMEM((npart // 128, 128), jnp.int32),
        pltpu.VMEM((2, npart), f32),
        pltpu.VMEM((npart // 128, 128), jnp.int32),
        pltpu.VMEM((npart // 128, 128), jnp.int32),
        pltpu.VMEM(observed_data.shape, f32),
        pltpu.VMEM((16 * NF, 128), f32),
        pltpu.VMEM((2, 16 * NF, 128), f32),
        pltpu.VMEM((2, 16, 128), f32),
        pltpu.VMEM((3, 2, 16, 128), f32),
        pltpu.VMEM((9, 64, 256), f32),
        pltpu.VMEM((3, 64, 256), f32),
        pltpu.VMEM((48, 128), f32),
        pltpu.VMEM((6 * STEPS, 16, 128), f32),
        pltpu.VMEM((6, 16, 128), f32),
        pltpu.VMEM((128, 128), f32),
        pltpu.VMEM((npart // 128, 128, 128), f32),
        pltpu.VMEM((npart // 128, 128), f32),
        pltpu.VMEM((128, npart), bf16),
        pltpu.VMEM((128, npart), bf16),
        pltpu.VMEM((32, 128), f32),
        pltpu.VMEM((16, 8, 128), f32),
        pltpu.VMEM((16, 8, 128), f32),
        pltpu.VMEM((64, 2, 128), f32),
        pltpu.VMEM((64, 2, 128), f32),
        pltpu.VMEM((128, 128), f32),
        pltpu.VMEM((128, 4096), bf16),
        pltpu.VMEM((16, 256), jnp.int32),
        pltpu.VMEM((64, 2, 128), f32),
        pltpu.VMEM((64, 2, 128), f32),
        pltpu.VMEM((16, 8, 128), f32),
        pltpu.VMEM((16, 8, 128), f32),
        pltpu.VMEM((128, 128), f32),
        pltpu.VMEM((2, 128, 128), f32),
        pltpu.VMEM((2, 8, 128), f32),
        pltpu.VMEM((3, 2, 8, 128), f32),
        pltpu.VMEM((3, 128, 128), f32),
        pltpu.VMEM((2 * STEPS, 64, 256), f32),
        dma((8,)),
        dma((8,)),
        dma((8,)),
        dma((8,)),
        dma((4,)),
        dma((4,)),
        dma((11,)),
        pltpu.SemaphoreType.REGULAR,
    ]
    residuals, gradients = pl.pallas_call(
        functools.partial(kernel, ngx, ngy, npart),
        out_shape=(
            jax.ShapeDtypeStruct(observed_data.shape, f32),
            jax.ShapeDtypeStruct((32, 128), f32),
        ),
        in_specs=[anywhere] * 11,
        out_specs=(pl.BlockSpec(memory_space=pltpu.VMEM),) * 2,
        scratch_shapes=scratch,
        compiler_params=pltpu.CompilerParams(collective_id=0, has_side_effects=True, vmem_limit_bytes=25165824),
        name="window",
    )(
        *[pltpu.with_memory_space_constraint(x, pltpu.HBM) for x in (
        initial_state.reshape(144, 128),
        lame_lambda.reshape(16, 128),
        shear_modulus.reshape(16, 128),
        buoyancy.reshape(16, 128),
        source_cells.reshape(1, nsrc),
        source_wavelet,
        segment_start.reshape(-1, 128),
        segment_weight,
        partial_owner.reshape(-1, 128),
        partial_channel.reshape(-1, 128),
        observed_data)],
    )
    residuals, gradients = pl.pallas_call(
        publish,
        out_shape=(jax.ShapeDtypeStruct(observed_data.shape, f32), jax.ShapeDtypeStruct((32, 128), f32)),
        in_specs=[anywhere, anywhere],
        out_specs=(anywhere, anywhere),
        scratch_shapes=[dma((2,))],
        compiler_params=pltpu.CompilerParams(vmem_limit_bytes=1 << 20),
        name="publish",
    )(residuals, gradients)
    return residuals, gradients.reshape(2, 4, 4, 128)


def solution(mesh):
    in_specs = (
        P(None, None, "gx", "gy"),
        P(None, "gx", "gy"),
        P(None, "gx", "gy"),
        P(None, "gx", "gy"),
        P(("gx", "gy")),
        P(None, ("gx", "gy")),
        P(("gx", "gy")),
        P(None, ("gx", "gy")),
        P(("gx", "gy"), None),
        P(("gx", "gy")),
        P(None, ("gx", "gy")),
    )
    out_specs = (P(None, ("gx", "gy")), P(None, None, "gx", "gy"))
    return jax.shard_map(shards, mesh=mesh, in_specs=in_specs, out_specs=out_specs, check_vma=False)
```

```python
import functools

import jax
import jax.numpy as jnp
from jax import lax
from jax.experimental import pallas as pl
from jax.experimental.pallas import tpu as pltpu
from jax.sharding import PartitionSpec as P

GAUGE = 8
DT = 0.25
PIECES = 3
STEPS = 3
NF = 14
MESH = pl.DeviceIdType.MESH
NT = (((1,), (1,)), ((), ()))
NN = (((1,), (0,)), ((), ()))


def iota(shape, dim):
    return lax.broadcasted_iota(jnp.int32, shape, dim)


def split(x):
    parts = []
    for _ in range(PIECES):
        part = x.astype(jnp.bfloat16)
        parts.append(part)
        x = x - part.astype(jnp.float32)
    return parts


def dot(a, b, dims):
    return lax.dot_general(a, b, dims, preferred_element_type=jnp.float32)


def dot_split(x, b, dims):
    parts = split(x)
    rows = x.shape[0]
    stacked = dot(jnp.concatenate(parts, axis=0), b, dims)
    total = stacked[:rows]
    for i in range(1, PIECES):
        total = total + stacked[i * rows : (i + 1) * rows]
    return total


def ones_where(mask):
    return jnp.where(mask, 1.0, 0.0).astype(jnp.bfloat16)


def narrow(x):
    return x.astype(jnp.float32).astype(jnp.bfloat16)


def spread_rows(x, key_rows, key, copies):
    hit = key_rows == narrow(key)
    zero = jnp.zeros(hit.shape, jnp.bfloat16)
    pieces = split(jnp.concatenate([x, x], axis=0))
    return jnp.concatenate(
        [jnp.where(hit, jnp.concatenate([piece] * copies, axis=0), zero) for piece in pieces], axis=0
    )


def ahead(f, axis):
    return pltpu.roll(f, f.shape[axis] - 1, axis) - f


def behind(f, axis):
    return f - pltpu.roll(f, 1, axis)


def time_step(ext, mats, emit):
    def plane(ref, f, z):
        return ref[f, pl.ds(16 * z, 16), :]

    def ahead_z(f, z):
        return (plane(ext, f, z + 1) if z < 3 else 0.0) - plane(ext, f, z)

    def behind_z(f, z):
        here = plane(ext, f, z)
        return here - plane(ext, f, z - 1) if z > 0 else here

    for z in range(4):
        scale = DT * plane(mats, 0, z)
        sxy, sxz, syz = plane(ext, 6, z), plane(ext, 7, z), plane(ext, 8, z)
        ax = ahead(plane(ext, 3, z), 0) + behind(sxy, 1) + behind_z(7, z)
        ay = behind(sxy, 0) + ahead(plane(ext, 4, z), 1) + behind_z(8, z)
        az = behind(sxz, 0) + behind(syz, 1) + ahead_z(5, z)
        for f, a in enumerate((ax, ay, az)):
            ext[f, pl.ds(16 * z, 16), :] = plane(ext, f, z) + scale * a
    for z in range(4):
        vx, vy, vz = plane(ext, 0, z), plane(ext, 1, z), plane(ext, 2, z)
        exx = behind(vx, 0)
        eyy = behind(vy, 1)
        ezz = behind_z(2, z)
        exy = ahead(vx, 1) + ahead(vy, 0)
        exz = ahead_z(0, z) + ahead(vz, 0)
        eyz = ahead_z(1, z) + ahead(vz, 1)
        emit(z, [e[4:8, 0:128] for e in (exx, eyy, ezz, exy, exz, eyz)])
        lam, mu = plane(mats, 1, z), plane(mats, 2, z)
        dil = lam * (exx + eyy + ezz)
        for f, e in ((3, exx), (4, eyy), (5, ezz)):
            ext[f, pl.ds(16 * z, 16), :] = plane(ext, f, z) + DT * (dil + 2.0 * mu * e)
        for f, e in ((6, exy), (7, exz), (8, eyz)):
            ext[f, pl.ds(16 * z, 16), :] = plane(ext, f, z) + DT * mu * e


def first_step(ext, mats, load_x, load_y, emit):
    def plane(ref, f, z):
        return ref[f, pl.ds(16 * z, 16), :]

    none = jnp.zeros((16, 256), jnp.float32)
    for z in range(4):
        rows = pl.ds(16 * z, 16)
        scale = DT * plane(mats, 0, z)
        ext[0, rows, :] = scale * ahead(load_x[rows, :], 0)
        ext[1, rows, :] = scale * ahead(load_y[rows, :], 1)
        ext[2, rows, :] = none
    for z in range(4):
        rows = pl.ds(16 * z, 16)
        vx, vy = plane(ext, 0, z), plane(ext, 1, z)
        exx = behind(vx, 0)
        eyy = behind(vy, 1)
        exy = ahead(vx, 1) + ahead(vy, 0)
        exz = (plane(ext, 0, z + 1) if z < 3 else 0.0) - vx
        eyz = (plane(ext, 1, z + 1) if z < 3 else 0.0) - vy
        emit(z, [e[4:8, 0:128] for e in (exx, eyy, none, exy, exz, eyz)])
        lam, mu = plane(mats, 1, z), plane(mats, 2, z)
        dil = lam * (exx + eyy)
        ext[3, rows, :] = load_x[rows, :] + DT * (dil + 2.0 * mu * exx)
        ext[4, rows, :] = load_y[rows, :] + DT * (dil + 2.0 * mu * eyy)
        ext[5, rows, :] = DT * dil
        for f, e in ((6, exy), (7, exz), (8, eyz)):
            ext[f, rows, :] = DT * mu * e


def kernel(
    ngx,
    ngy,
    npart,
    state_in,
    lam_in,
    mu_in,
    buoy_in,
    scell_in,
    swave_in,
    start_in,
    weight_in,
    owner_in,
    chan_in,
    obs_in,
    res_out,
    grad_out,
    scell,
    swave,
    start,
    weight,
    owner,
    chan,
    obs,
    own,
    xr,
    strip,
    yr,
    ext,
    mats,
    srcs,
    es,
    ad,
    glhs,
    colb,
    rank,
    win,
    lane1h,
    obs32,
    sa,
    ra,
    sx,
    rx,
    arr,
    chan1h,
    hirow,
    sx2,
    rx2,
    sa2,
    ra2,
    load,
    xr2,
    strip2,
    yr2,
    halo2,
    exl,
    hsend,
    hrecv,
    h2send,
    h2recv,
    esend,
    erecv,
    isem,
    ready,
):
    gx, gy = lax.axis_index("gx"), lax.axis_index("gy")
    nchunk = npart // 128
    gy_bits = ngy.bit_length() - 1
    y_bits = gy_bits // 2
    ny = 1 << y_bits
    nx = ngy // ny
    right_x, left_x = lax.rem(gx + 1, ngx), lax.rem(gx + ngx - 1, ngx)
    right_y, left_y = lax.rem(gy + 1, ngy), lax.rem(gy + ngy - 1, ngy)
    first_x, last_x = gx == 0, gx == ngx - 1
    first_y, last_y = gy == 0, gy == ngy - 1

    if ngx < 16 or ngy < 64:
        for ref in (ra, rx, rx2, ra2):
            ref[...] = jnp.zeros_like(ref)

    barrier = pltpu.get_barrier_semaphore()

    def greet(x, y):
        pl.semaphore_signal(barrier, inc=1, device_id={"gx": x, "gy": y}, device_id_type=MESH)

    reads = [
        pltpu.make_async_copy(src, dst, isem.at[i])
        for i, (src, dst) in enumerate(
            (
                (state_in, own.at[pl.ds(0, 144)]),
                (scell_in, scell),
                (swave_in, swave),
                (buoy_in, own.at[pl.ds(144, 16)]),
                (lam_in, own.at[pl.ds(160, 16)]),
                (mu_in, own.at[pl.ds(176, 16)]),
                (owner_in, owner),
                (start_in, start),
                (chan_in, chan),
                (weight_in, weight),
                (obs_in, obs),
            )
        )
    ]
    for read in reads:
        read.start()

    def far_first(count):
        return sorted(range(1, count), key=lambda i: -min(i, count - i))

    def peer_z(i):
        return lax.rem(gx + i, ngx), gy

    def peer_x(i):
        return gx, lax.rem((gy >> y_bits) + i, nx) * ny + (gy & (ny - 1))

    def peer_y(i):
        return gx, (gy & ~(ny - 1)) + lax.rem((gy & (ny - 1)) + i, ny)

    greeted = [peer_z(i) for i in far_first(ngx)] + [peer_x(i) for i in far_first(nx)] + [peer_y(i) for i in far_first(ny)]
    greeted += [(x, y) for y in (left_y, right_y) for x in (gx, left_x, right_x)]
    for x, y in greeted:
        greet(x, y)

    mats[...] = jnp.zeros_like(mats)
    ext[...] = jnp.zeros_like(ext)
    exl[...] = jnp.zeros_like(exl)
    glhs[...] = jnp.zeros_like(glhs)
    obs32[...] = jnp.zeros_like(obs32)
    for read in reads[:7]:
        read.wait()

    cell = scell[...]
    nsrc = cell.shape[1]
    key = iota((48, nsrc), 0)
    wave = jnp.concatenate([jnp.broadcast_to(swave[t : t + 1, :], (16, nsrc)) for t in range(STEPS)], axis=0)
    lhs = jnp.where((key & 15) == (cell >> 7), wave, 0.0)
    srcs[...] = dot_split(lhs, ones_where(iota((128, nsrc), 0) == (cell & 127)), NT)
    for f in (3, 4, 5):
        own[16 * f : 16 * f + 16, :] = own[16 * f : 16 * f + 16, :] + srcs[0:16, :]
    own[192:224, :] = srcs[16:48, :]

    lane = iota((8, 128), 1)
    sub = iota((8, 128), 0)
    low4 = (lane & 7) < 4

    def pack(tile_of, groups, put):
        for u in range(-(-groups // 16)):
            acc = [jnp.zeros((8, 128), jnp.float32)] * 2
            for k in range(min(16, groups - 16 * u)):
                tile = tile_of(16 * u + k)
                here = (lane >> 3) == k
                acc[0] = jnp.where(here, pltpu.roll(tile, (8 * k - 124) % 128, 1), acc[0])
                acc[1] = jnp.where(here, pltpu.roll(tile, (8 * k + 4) % 128, 1), acc[1])
            for side in range(2):
                put(side, u, acc[side])

    def put_strip(side, u, value):
        strip[side, pl.ds(8 * u, 8), :] = value

    pack(lambda i: own[8 * i : 8 * i + 8, :], 2 * NF, put_strip)

    ownf = owner[...].astype(jnp.float32)
    cols = jnp.concatenate([ownf, jnp.zeros((128 - nchunk, 128), jnp.float32)], axis=0).T
    for c in range(nchunk):
        colb[c] = jnp.broadcast_to(cols[:, c : c + 1], (128, 128))
    earlier = iota((128, 128), 0) < iota((128, 128), 1)

    def rank_chunk(c):
        row = jnp.broadcast_to(owner[pl.ds(c, 1), :].astype(jnp.float32), (128, 128))
        same = jnp.where((colb[c] == row) & earlier, 1.0, 0.0)

        def more(q, count):
            hit = jnp.where(colb[q] == row, 1.0, 0.0)
            return count + hit.reshape(16, 8, 128).sum(axis=0)

        count = lax.fori_loop(0, c, more, same.reshape(16, 8, 128).sum(axis=0))
        rank[pl.ds(c, 1), :] = jnp.sum(count, axis=0, keepdims=True)

    halfway = nchunk * 11 // 16
    pl.loop(0, halfway)(rank_chunk)

    pl.semaphore_wait(barrier, len(greeted))
    for i in far_first(nx):
        x, y = peer_x(i)
        pl.semaphore_signal(ready, inc=1, device_id={"gx": x, "gy": y}, device_id_type=MESH)

    def halo_copies(rows, rows_to, strips, strips_to, send, recv):
        plan = [
            (strips.at[0], strips_to.at[0, 0], right_x, right_y),
            (strips.at[1], strips_to.at[0, 1], right_x, left_y),
            (strips.at[0], strips_to.at[2, 0], left_x, right_y),
            (strips.at[1], strips_to.at[2, 1], left_x, left_y),
            (strips.at[0], strips_to.at[1, 0], gx, right_y),
            (strips.at[1], strips_to.at[1, 1], gx, left_y),
            (rows, rows_to.at[0], right_x, gy),
            (rows, rows_to.at[1], left_x, gy),
        ]
        copies = [
            pltpu.make_async_remote_copy(
                src_ref=src,
                dst_ref=dst,
                send_sem=send.at[i],
                recv_sem=recv.at[i],
                device_id={"gx": x, "gy": y},
                device_id_type=MESH,
            )
            for i, (src, dst, x, y) in enumerate(plan)
        ]
        for copy in copies:
            copy.start()
        return copies

    copies = halo_copies(own, xr, strip, yr, hsend, hrecv)
    for read in reads[7:]:
        read.wait()

    pl.loop(halfway, nchunk)(rank_chunk)

    for i in range(8):
        obs32[4 * i : 4 * i + 3, :] = obs[:, 128 * i : 128 * i + 128]


    def chunk_key(c, width):
        own_c = jnp.concatenate([owner[c + i : c + i + 1, :] for i in range(width)], axis=1)
        rank_c = jnp.concatenate([rank[c + i : c + i + 1, :] for i in range(width)], axis=1).astype(jnp.int32)
        return own_c, rank_c

    def row_of(c, width):
        start_c = jnp.concatenate([start[c + i : c + i + 1, :] for i in range(width)], axis=1)
        row_c = (start_c * 8666) >> 20
        return start_c, row_c

    for c in range(nchunk):
        start_c, row_c = row_of(c, 1)
        ahead_c = iota((128, 128), 0) - (start_c - 121 * row_c)
        win[:, 128 * c : 128 * c + 128] = ones_where((ahead_c >= 0) & (ahead_c < GAUGE))
        own_c, rank_c = chunk_key(c, 1)
        lane_c = (own_c & (ngy - 1)) * 2 + (rank_c & 1)
        lane1h[:, 128 * c : 128 * c + 128] = ones_where(iota((128, 128), 0) == lane_c)

    def place_rows(g, rows_ref, drop):
        for f in range(NF):
            for z in range(4):
                part = rows_ref[16 * f + 4 * z : 16 * f + 4 * z + 4, :]
                if drop is not None:
                    part = jnp.where(drop, 0.0, part)
                put_ext(f, slice(16 * z + 4 * g, 16 * z + 4 * g + 4), slice(0, 128), part)

    def put_ext(f, rows, lanes, value):
        if f < 9:
            ext[f, rows, lanes] = value
        elif f < 12:
            mats[f - 9, rows, lanes] = value
        else:
            exl[f - 12, rows, lanes] = value

    def comb(strips, g, u):
        low = jnp.where(first_y, 0.0, strips[g, 0, pl.ds(8 * u, 8), :])
        high = jnp.where(last_y, 0.0, strips[g, 1, pl.ds(8 * u, 8), :])
        both = jnp.where(low4, low, high)
        if g == 0:
            both = jnp.where(first_x, 0.0, both)
        if g == 2:
            both = jnp.where(last_x, 0.0, both)
        return both

    place_rows(1, own, None)
    for copy in copies:
        copy.wait()
    place_rows(0, xr.at[0], first_x)
    place_rows(2, xr.at[1], last_x)
    for g in range(3):
        for u in range(2):
            both = comb(yr, g, u)
            for k in range(min(16, 2 * NF - 16 * u)):
                f, h = divmod(16 * u + k, 2)
                tile = pltpu.roll(both, (124 - 8 * k) % 128, 1)
                for i in range(2):
                    z = 2 * h + i
                    put_ext(f, slice(16 * z + 4 * g, 16 * z + 4 * g + 4), slice(128, 256), tile[4 * i : 4 * i + 4, :])

    for t in range(STEPS):
        if t > 0:
            for f in (3, 4, 5):
                ext[f] = ext[f] + exl[t - 1]

        def emit(z, e, t=t):
            for i in range(6):
                es[6 * t + i, pl.ds(4 * z, 4), :] = e[i]
            for f in range(2):
                glhs[pl.ds(32 * z + 4 * f + t, 4, stride=8), :] = e[f]

        time_step(ext, mats, emit)

    def sub_of(width):
        return iota((8, width), 0)

    def weights(c, width):
        both = weight[:, 128 * c : 128 * (c + width)]
        return jnp.where(sub_of(128 * width) < 4, both[0:1, :], both[1:2, :])

    width = 2 if nchunk % 2 == 0 else 1
    wide = 128 * width
    by_four, by_eight = narrow(iota((128, wide), 0) >> 2), narrow(iota((128, wide), 0) >> 3)
    gpieces = jnp.concatenate(split(glhs[...]), axis=0)
    acc = jnp.zeros((PIECES * 128, 128), jnp.float32)
    for c in range(0, nchunk, width):
        lanes = slice(128 * c, 128 * c + wide)
        _, row_c = row_of(c, width)
        got = dot(gpieces, win[:, lanes], NN)
        picked = jnp.zeros((8, wide), jnp.float32)
        for r in range(16):
            tile = got[8 * r : 8 * r + 8]
            for i in range(1, PIECES):
                tile = tile + got[128 * i + 8 * r : 128 * i + 8 * r + 8]
            picked = picked + jnp.where(row_c == r, tile, 0.0)
        picked = picked * weights(c, width)
        picked = picked + pltpu.roll(picked, 4, 0)
        chan_c = jnp.concatenate([chan[c + i : c + i + 1, :] for i in range(width)], axis=1)
        picked = jnp.where((sub_of(wide) & 3) == 3, chan_c.astype(jnp.float32), picked)
        own_c, rank_c = chunk_key(c, width)
        key_c = (own_c >> gy_bits) * 2 + (rank_c >> 1)
        acc = acc + dot(spread_rows(picked, by_four, key_c, 8), lane1h[:, lanes], NT)
    total = acc[0:128]
    for i in range(1, PIECES):
        total = total + acc[128 * i : 128 * i + 128]
    sa[...] = total.reshape(16, 8, 128)

    def exchange(stage, peers, me, src, dst):
        send, recv = esend.at[stage], erecv.at[stage]
        for place, x, y in peers:
            pltpu.make_async_remote_copy(
                src_ref=src.at[place],
                dst_ref=dst.at[me],
                send_sem=send,
                recv_sem=recv,
                device_id={"gx": x, "gy": y},
                device_id_type=MESH,
            ).start()
        pltpu.make_async_copy(src.at[me], dst.at[me], recv).start()
        whole, less = dst.at[pl.ds(0, len(peers) + 1)], src.at[pl.ds(0, len(peers))]
        pltpu.make_async_copy(whole, whole, recv).wait()
        pltpu.make_async_copy(less, less, send).wait()

    z_peers = [(lax.rem(gx + i, ngx), lax.rem(gx + i, ngx), gy) for i in far_first(ngx)]
    xs = [lax.rem((gy >> y_bits) + i, nx) * ny for i in range(nx)]
    ys = [lax.rem((gy & (ny - 1)) + i, ny) for i in range(ny)]
    offsets = [(i, j) for i in range(nx) for j in range(ny) if i or j]
    offsets.sort(key=lambda o: -min(o[0], nx - o[0]) - min(o[1], ny - o[1]))
    xy_peers = [(xs[i] + ys[j], gx, xs[i] + ys[j]) for i, j in offsets]

    exchange(0, z_peers, gx, sa, ra)
    sx[...] = ra[...].reshape(128, 128).T.reshape(64, 2, 128)
    pl.semaphore_wait(ready, nx - 1)
    exchange(1, xy_peers, gy, sx, rx)
    arr[...] = rx[...].reshape(128, 128).T

    acc = jnp.zeros((PIECES * 32, 128), jnp.float32)
    sub256 = sub_of(256) >> 2
    rows256 = narrow(iota((128, 256), 0))
    one, none = jnp.ones((128, 256), jnp.bfloat16), jnp.zeros((128, 256), jnp.bfloat16)
    by_four32 = narrow(iota((32, 256), 0) >> 2)
    for d in range(16):
        tile = arr[8 * d : 8 * d + 8, :]
        turned = pltpu.roll(tile, 4, 0)
        both = jnp.concatenate([jnp.where(sub < 4, tile, turned), jnp.where(sub < 4, turned, tile)], axis=1)
        ids = both[3:4, :].astype(jnp.int32)
        onehot = jnp.where(rows256 == narrow(ids & 127), one, none)
        chan1h[:, 256 * d : 256 * d + 256] = onehot
        hi = ids >> 7
        hirow[d : d + 1, :] = hi
        acc = acc + dot(spread_rows(both, by_four32, hi, 2), onehot, NT)
    sums = acc[0:32]
    for i in range(1, PIECES):
        sums = sums + acc[32 * i : 32 * i + 32]
    sums = jnp.where((iota((32, 128), 0) & 3) == 3, 0.0, sums - obs32[...])
    for i in range(8):
        res_out[:, 128 * i : 128 * i + 128] = sums[4 * i : 4 * i + 3, :]

    pieces = jnp.concatenate(split(sums), axis=0)
    for d in range(16):
        got = dot(pieces, chan1h[:, 256 * d : 256 * d + 256], NN)
        hi = hirow[d : d + 1, :]
        picked = jnp.zeros((8, 256), jnp.float32)
        for j in range(4):
            tile = got[8 * j : 8 * j + 8]
            for i in range(1, PIECES):
                tile = tile + got[32 * i + 8 * j : 32 * i + 8 * j + 8]
            picked = picked + jnp.where(hi == sub256 + 2 * j, tile, 0.0)
        picked = picked + pltpu.roll(picked, 4, 0)
        arr[8 * d : 8 * d + 8, :] = jnp.where(sub < 4, picked[:, 0:128], picked[:, 128:256])
    sx2[...] = arr[...].T.reshape(64, 2, 128)
    exchange(2, xy_peers, gy, sx2, rx2)
    sa2[...] = rx2[...].reshape(128, 128).T.reshape(16, 8, 128)
    exchange(3, z_peers, gx, sa2, ra2)

    pieces = jnp.concatenate(split(ra2[...].reshape(128, 128)), axis=0)
    acc = jnp.zeros((PIECES * 128, 128), jnp.float32)
    for c in range(0, nchunk, width):
        lanes = slice(128 * c, 128 * c + wide)
        got = dot(pieces, lane1h[:, lanes], NN)
        own_c, rank_c = chunk_key(c, width)
        key_c = (own_c >> gy_bits) * 2 + (rank_c >> 1)
        half = sub_of(wide) >> 2
        picked = jnp.zeros((8, wide), jnp.float32)
        for r in range(16):
            tile = got[8 * r : 8 * r + 8]
            for i in range(1, PIECES):
                tile = tile + got[128 * i + 8 * r : 128 * i + 8 * r + 8]
            picked = picked + jnp.where(key_c == half + 2 * r, tile, 0.0)
        picked = (picked + pltpu.roll(picked, 4, 0)) * weights(c, width)
        _, row_c = row_of(c, width)
        acc = acc + dot(spread_rows(picked, by_eight, row_c, 8), win[:, lanes], NT)
    total = acc[0:128]
    for i in range(1, PIECES):
        total = total + acc[128 * i : 128 * i + 128]
    load[...] = total

    def put_strip2(side, u, value):
        strip2[side] = value

    pack(lambda i: load[8 * i : 8 * i + 8, :], 16, put_strip2)
    copies = halo_copies(load, xr2, strip2, yr2, h2send, h2recv)

    def place_loads(g, ref, drop):
        for f in range(2):
            for t in range(STEPS):
                for z in range(4):
                    part = ref[pl.ds(32 * z + 4 * f + t, 4, stride=8), :]
                    if drop is not None:
                        part = jnp.where(drop, 0.0, part)
                    exl[2 * t + f, 16 * z + 4 * g : 16 * z + 4 * g + 4, 0:128] = part

    place_loads(1, load, None)
    for copy in copies:
        copy.wait()
    place_loads(0, xr2.at[0], first_x)
    place_loads(2, xr2.at[1], last_x)
    for g in range(3):
        both = comb(yr2, g, 0)
        for k in range(16):
            halo2[g, pl.ds(8 * k, 8), :] = pltpu.roll(both, (124 - 8 * k) % 128, 1)
    for f in range(2):
        for t in range(STEPS):
            for z in range(4):
                rows = pl.ds(32 * z + 4 * f + t, 4, stride=8)
                for g in range(3):
                    exl[2 * t + f, 16 * z + 4 * g : 16 * z + 4 * g + 4, 128:256] = halo2[g, rows, :]

    lam_grad = jnp.zeros((16, 128), jnp.float32)
    mu_grad = jnp.zeros((16, 128), jnp.float32)
    for k in range(STEPS):
        t = STEPS - 1 - k

        def emit(z, e):
            for i in range(6):
                ad[i, pl.ds(4 * z, 4), :] = e[i]

        if k == 0:
            first_step(ext, mats, exl.at[2 * t], exl.at[2 * t + 1], emit)
        else:
            for f in range(2):
                ext[3 + f] = ext[3 + f] + exl[2 * t + f]
            time_step(ext, mats, emit)
        fwd = [es[6 * t + i] for i in range(6)]
        adj = [ad[i] for i in range(6)]
        prod = [a * b for a, b in zip(fwd, adj)]
        lam_grad = lam_grad + (fwd[0] + fwd[1] + fwd[2]) * (adj[0] + adj[1] + adj[2])
        mu_grad = mu_grad + (2.0 * (prod[0] + prod[1] + prod[2]) + prod[3] + prod[4] + prod[5])
    grad_out[0:16, :] = lam_grad
    grad_out[16:32, :] = mu_grad


def publish(res_in, grad_in, res_out, grad_out, sem):
    copies = [
        pltpu.make_async_copy(res_in, res_out, sem.at[0]),
        pltpu.make_async_copy(grad_in, grad_out, sem.at[1]),
    ]
    for copy in copies:
        copy.start()
    for copy in copies:
        copy.wait()


def shards(
    initial_state,
    lame_lambda,
    shear_modulus,
    buoyancy,
    source_cells,
    source_wavelet,
    segment_start,
    segment_weight,
    partial_owner,
    partial_channel,
    observed_data,
):
    ngx, ngy = lax.axis_size("gx"), lax.axis_size("gy")
    npart = segment_start.shape[0]
    nsrc = source_cells.shape[0]
    f32, bf16 = jnp.float32, jnp.bfloat16
    anywhere = pl.BlockSpec(memory_space=pl.ANY)
    dma = pltpu.SemaphoreType.DMA
    scratch = [
        pltpu.VMEM((1, nsrc), jnp.int32),
        pltpu.VMEM((STEPS, nsrc), f32),
        pltpu.VMEM((npart // 128, 128), jnp.int32),
        pltpu.VMEM((2, npart), f32),
        pltpu.VMEM((npart // 128, 128), jnp.int32),
        pltpu.VMEM((npart // 128, 128), jnp.int32),
        pltpu.VMEM(observed_data.shape, f32),
        pltpu.VMEM((16 * NF, 128), f32),
        pltpu.VMEM((2, 16 * NF, 128), f32),
        pltpu.VMEM((2, 16, 128), f32),
        pltpu.VMEM((3, 2, 16, 128), f32),
        pltpu.VMEM((9, 64, 256), f32),
        pltpu.VMEM((3, 64, 256), f32),
        pltpu.VMEM((48, 128), f32),
        pltpu.VMEM((6 * STEPS, 16, 128), f32),
        pltpu.VMEM((6, 16, 128), f32),
        pltpu.VMEM((128, 128), f32),
        pltpu.VMEM((npart // 128, 128, 128), f32),
        pltpu.VMEM((npart // 128, 128), f32),
        pltpu.VMEM((128, npart), bf16),
        pltpu.VMEM((128, npart), bf16),
        pltpu.VMEM((32, 128), f32),
        pltpu.VMEM((16, 8, 128), f32),
        pltpu.VMEM((16, 8, 128), f32),
        pltpu.VMEM((64, 2, 128), f32),
        pltpu.VMEM((64, 2, 128), f32),
        pltpu.VMEM((128, 128), f32),
        pltpu.VMEM((128, 4096), bf16),
        pltpu.VMEM((16, 256), jnp.int32),
        pltpu.VMEM((64, 2, 128), f32),
        pltpu.VMEM((64, 2, 128), f32),
        pltpu.VMEM((16, 8, 128), f32),
        pltpu.VMEM((16, 8, 128), f32),
        pltpu.VMEM((128, 128), f32),
        pltpu.VMEM((2, 128, 128), f32),
        pltpu.VMEM((2, 8, 128), f32),
        pltpu.VMEM((3, 2, 8, 128), f32),
        pltpu.VMEM((3, 128, 128), f32),
        pltpu.VMEM((2 * STEPS, 64, 256), f32),
        dma((8,)),
        dma((8,)),
        dma((8,)),
        dma((8,)),
        dma((4,)),
        dma((4,)),
        dma((11,)),
        pltpu.SemaphoreType.REGULAR,
    ]
    residuals, gradients = pl.pallas_call(
        functools.partial(kernel, ngx, ngy, npart),
        out_shape=(
            jax.ShapeDtypeStruct(observed_data.shape, f32),
            jax.ShapeDtypeStruct((32, 128), f32),
        ),
        in_specs=[anywhere] * 11,
        out_specs=(pl.BlockSpec(memory_space=pltpu.VMEM),) * 2,
        scratch_shapes=scratch,
        compiler_params=pltpu.CompilerParams(collective_id=0, has_side_effects=True, vmem_limit_bytes=25165824),
        name="window",
    )(
        *[pltpu.with_memory_space_constraint(x, pltpu.HBM) for x in (
        initial_state.reshape(144, 128),
        lame_lambda.reshape(16, 128),
        shear_modulus.reshape(16, 128),
        buoyancy.reshape(16, 128),
        source_cells.reshape(1, nsrc),
        source_wavelet,
        segment_start.reshape(-1, 128),
        segment_weight,
        partial_owner.reshape(-1, 128),
        partial_channel.reshape(-1, 128),
        observed_data)],
    )
    residuals, gradients = pl.pallas_call(
        publish,
        out_shape=(jax.ShapeDtypeStruct(observed_data.shape, f32), jax.ShapeDtypeStruct((32, 128), f32)),
        in_specs=[anywhere, anywhere],
        out_specs=(anywhere, anywhere),
        scratch_shapes=[dma((2,))],
        compiler_params=pltpu.CompilerParams(vmem_limit_bytes=1 << 20),
        name="publish",
    )(residuals, gradients)
    return residuals, gradients.reshape(2, 4, 4, 128)


def solution(mesh):
    in_specs = (
        P(None, None, "gx", "gy"),
        P(None, "gx", "gy"),
        P(None, "gx", "gy"),
        P(None, "gx", "gy"),
        P(("gx", "gy")),
        P(None, ("gx", "gy")),
        P(("gx", "gy")),
        P(None, ("gx", "gy")),
        P(("gx", "gy"), None),
        P(("gx", "gy")),
        P(None, ("gx", "gy")),
    )
    out_specs = (P(None, ("gx", "gy")), P(None, None, "gx", "gy"))
    return jax.shard_map(shards, mesh=mesh, in_specs=in_specs, out_specs=out_specs, check_vma=False)
```
